32 devices in a mesh: depth: 8 (over z, x), stripe: 4 (over y, core).
Axes of the slice: x: 2, y: 2, z: 4, core: 2. Of those that a mesh axis runs over, the one named last changes fastest.
Arguments:
- object_slices: float32 [8, 2, 1024, 384], P('depth', None, 'stripe'), may hold values from -1 to 1, as said below
- probe_wave: bfloat16 [2, 256, 256], replicated, may hold values from -5 to 5
- amplitudes: bfloat16 [16, 256, 256], P('stripe'), may hold values from 0 to 2
- positions: int32 [16, 2], replicated, may hold values from 0 to 255, as said below
- counts: int32 [4], replicated, may hold values from 1 to 4, as said below
Outputs:
- grad_object: float32 [8, 2, 1024, 384], P('depth', None, 'stripe')
The draws below stay inside these ranges and needn't reach their ends.
Inputs may be any that keep to these rules, and one draw needn't show every extreme that they name: `object_slices`: every cell has magnitude at most 1. `positions`: row offsets lie in 0 to 255 and column offsets in 0 to 128. The counts sum to 8 and the largest equals 4; a stripe's live slots are its first ones.
All inputs are finite; a program needn't handle non-finite values.
Results may differ from the reference program's by a relative error of at most 0.0003.
Values may be sent and summed in bfloat16 or wider, within the bound.
A program may use at most 64 MiB of HBM per device.

```python
import math
import jax
import jax.numpy as jnp
from jax import lax

WIN = 256
STRIPE_ROWS = 256
W = 384
CAP = 4
SLICES = 8
ROWS_ALL = 1024
SLOTS = 16
TOTAL = 8
N_STRIPE = 4


def draw_object_slices(key, part):
    key_mag, key_phase = jax.random.split(jax.random.fold_in(key, 11))
    shape = (SLICES, ROWS_ALL, W)
    magnitude = jax.random.uniform(key_mag, shape, jnp.float32, 0.97, 1.0)
    phase_angle = jax.random.uniform(key_phase, shape, jnp.float32, -math.pi, math.pi)
    return jnp.stack([magnitude * jnp.cos(phase_angle), magnitude * jnp.sin(phase_angle)], axis=1).astype(jnp.float32)


def draw_positions(key, part):
    key_row, key_col, key_cross = jax.random.split(jax.random.fold_in(key, 23), 3)
    rows_drawn = jax.random.randint(key_row, (SLOTS,), 0, STRIPE_ROWS, jnp.int32)
    cols_drawn = jax.random.randint(key_col, (SLOTS,), 0, W - WIN + 1, jnp.int32)
    crossing = jax.random.randint(key_cross, (N_STRIPE,), STRIPE_ROWS - WIN // 2, STRIPE_ROWS, jnp.int32)
    first_slots = jnp.arange(N_STRIPE, dtype=jnp.int32) * CAP
    rows_drawn = rows_drawn.at[first_slots].set(crossing)
    rows_drawn = rows_drawn.at[0].set(STRIPE_ROWS - 1)
    cols_drawn = cols_drawn.at[0].set(W - WIN).at[1].set(0)
    return jnp.stack([rows_drawn, cols_drawn], axis=1).astype(jnp.int32)


def draw_counts(key, part):
    key_fill, key_turn = jax.random.split(jax.random.fold_in(key, 37))
    spare_units = (N_STRIPE - 1) * (CAP - 1)
    drawn_units = TOTAL - CAP - (N_STRIPE - 1)
    unit_order = jax.random.permutation(key_fill, spare_units)
    chosen = unit_order[:drawn_units] // (CAP - 1)
    added_units = jnp.sum((chosen[:, None] == jnp.arange(N_STRIPE - 1, dtype=jnp.int32)[None, :]).astype(jnp.int32), axis=0)
    rest_counts = (1 + added_units).astype(jnp.int32)
    full_counts = jnp.concatenate([jnp.full((1,), CAP, jnp.int32), rest_counts])
    rotation = jax.random.randint(key_turn, (), 0, N_STRIPE, jnp.int32)
    return jnp.roll(full_counts, rotation).astype(jnp.int32)


def levels(rng, dims, pieces, smallest, largest):
    gain, own = 1.0, jax.random.fold_in(rng, 6)
    for position, blocks in pieces:
        heights = jnp.exp(jax.random.uniform(jax.random.fold_in(own, position), (blocks,), jnp.float32, smallest / len(pieces), largest / len(pieces)))
        gain = gain * jnp.repeat(heights, dims[position] // blocks).reshape([-1 if axis == position else 1 for axis in range(len(dims))])
    return gain


def bell_draw(own_key, extent, scale, most, kind=jnp.bfloat16):
    values = scale * jax.random.normal(own_key, extent, jnp.float32)
    return jnp.clip(values, min=-most, max=most).astype(kind)


def setup_inputs(seed: int = 0) -> dict:
    streams_of = jax.random.split(jax.random.key(seed), 6)
    object_slices = draw_object_slices(jax.random.fold_in(streams_of[5], 71), 0)
    probe_wave = bell_draw(streams_of[1], (2, WIN, WIN), 0.7, 5.0)
    amplitudes = jnp.clip(2.0 * jax.random.uniform(streams_of[2], (SLOTS, WIN, WIN), jnp.float32) ** levels(streams_of[2], (SLOTS, WIN, WIN), ((0, 4),), -0.2, 0.2), 0.0, 2.0).astype(jnp.bfloat16)
    positions = draw_positions(jax.random.fold_in(streams_of[5], 71), 0)
    counts = draw_counts(jax.random.fold_in(streams_of[5], 71), 0)
    return {"object_slices": object_slices, "probe_wave": probe_wave, "amplitudes": amplitudes, "positions": positions, "counts": counts}


smoothing = 0.25
highest = lax.Precision.HIGHEST

def make_tables(length):
    index_row = jnp.arange(length, dtype=jnp.int32)
    product = index_row[:, None] * index_row[None, :] % length
    angle = 2.0 * math.pi * product.astype(jnp.float32) / length
    scale = 1.0 / math.sqrt(length)
    cos_part = (jnp.cos(angle) * scale).astype(jnp.float32)
    sin_part = (-jnp.sin(angle) * scale).astype(jnp.float32)
    neg_part = (jnp.sin(angle) * scale).astype(jnp.float32)
    right_fwd = jnp.concatenate([cos_part, sin_part], axis=1)
    left_fwd = jnp.concatenate([cos_part, sin_part], axis=0)
    right_inv = jnp.concatenate([cos_part, neg_part], axis=1)
    left_inv = jnp.concatenate([cos_part, neg_part], axis=0)
    freq = ((index_row + length // 2) % length - length // 2).astype(jnp.float32)
    phase = -math.pi * (freq[:, None] * freq[:, None] + freq[None, :] * freq[None, :]) / (2.0 * length)
    return (right_fwd, left_fwd, right_inv, left_inv, jnp.cos(phase), jnp.sin(phase))

def transform(real_in, imag_in, right_tab, left_tab):
    length = real_in.shape[0]
    stacked = jnp.concatenate([real_in, imag_in], axis=0)
    first_pass = jnp.dot(stacked, right_tab, precision=highest, preferred_element_type=jnp.float32)
    mid_real = first_pass[:length, :length] - first_pass[length:, length:]
    mid_imag = first_pass[:length, length:] + first_pass[length:, :length]
    second = jnp.dot(left_tab, jnp.concatenate([mid_real, mid_imag], axis=1), precision=highest, preferred_element_type=jnp.float32)
    out_real = second[:length, :length] - second[length:, length:]
    out_imag = second[:length, length:] + second[length:, :length]
    return (out_real, out_imag)

def transmit(wave_in, window):
    real_t = wave_in[0] * window[0] - wave_in[1] * window[1]
    imag_t = wave_in[0] * window[1] + wave_in[1] * window[0]
    return (real_t, imag_t)

def advance(wave_in, window, tables):
    right_fwd, left_fwd, right_inv, left_inv, prop_cos, prop_sin = tables
    real_t, imag_t = transmit(wave_in, window)
    spec_real, spec_imag = transform(real_t, imag_t, right_fwd, left_fwd)
    prop_real = spec_real * prop_cos - spec_imag * prop_sin
    prop_imag = spec_real * prop_sin + spec_imag * prop_cos
    out_real, out_imag = transform(prop_real, prop_imag, right_inv, left_inv)
    return jnp.stack([out_real, out_imag])

def exit_adjoint(wave_in, window, amplitude, tables):
    right_fwd, left_fwd = (tables[0], tables[1])
    real_t, imag_t = transmit(wave_in, window)
    far_real, far_imag = transform(real_t, imag_t, right_fwd, left_fwd)
    smooth = jnp.sqrt(far_real * far_real + far_imag * far_imag + smoothing)
    factor = 1.0 - amplitude.astype(jnp.float32) / smooth
    return jnp.stack([factor * far_real, factor * far_imag])

def unfold(adjoint, tables):
    out_real, out_imag = transform(adjoint[0], adjoint[1], tables[2], tables[3])
    return jnp.stack([out_real, out_imag])

def retreat(adjoint, tables):
    right_fwd, left_fwd, right_inv, left_inv, prop_cos, prop_sin = tables
    spec_real, spec_imag = transform(adjoint[0], adjoint[1], right_fwd, left_fwd)
    back_real = spec_real * prop_cos + spec_imag * prop_sin
    back_imag = spec_imag * prop_cos - spec_real * prop_sin
    out_real, out_imag = transform(back_real, back_imag, right_inv, left_inv)
    return jnp.stack([out_real, out_imag])

def slice_grad(wave_in, middle):
    return jnp.stack([wave_in[0] * middle[0] + wave_in[1] * middle[1], wave_in[0] * middle[1] - wave_in[1] * middle[0]])

def back_wave(window, middle):
    return jnp.stack([window[0] * middle[0] + window[1] * middle[1], window[0] * middle[1] - window[1] * middle[0]])

def reference(object_slices, probe_wave, amplitudes, positions, counts):
    tables = make_tables(WIN)
    total_rows = object_slices.shape[2]
    padded = jnp.concatenate([object_slices, object_slices[:, :, :WIN]], axis=2)
    zero_index = jnp.zeros((), jnp.int32)
    probe_float = probe_wave.astype(jnp.float32)

    def one_slot(gradient, slot_id):
        stripe_id = slot_id // CAP
        is_live = slot_id % CAP < counts[stripe_id]
        row_start = (stripe_id * STRIPE_ROWS + positions[slot_id, 0]).astype(jnp.int32)
        col_start = positions[slot_id, 1].astype(jnp.int32)
        corner = (zero_index, zero_index, row_start, col_start)

        def slot_work(gradient):
            windows = lax.dynamic_slice(padded, corner, (SLICES, 2, WIN, WIN))

            def forward_layer(wave_in, window):
                return (advance(wave_in, window, tables), wave_in)
            last_in, inputs = lax.scan(forward_layer, probe_float, windows[:-1])
            far_adj = exit_adjoint(last_in, windows[-1], amplitudes[slot_id], tables)
            middle = unfold(far_adj, tables)
            grad_last = slice_grad(last_in, middle)
            adjoint = back_wave(windows[-1], middle)

            def backward_layer(adjoint, pair_in):
                window, wave_in = pair_in
                middle = retreat(adjoint, tables)
                return (back_wave(window, middle), slice_grad(wave_in, middle))
            _, slice_grads = lax.scan(backward_layer, adjoint, (windows[:-1], inputs), reverse=True)
            all_grads = jnp.concatenate([slice_grads, grad_last[None]], axis=0)
            region = lax.dynamic_slice(gradient, corner, (SLICES, 2, WIN, WIN))
            return lax.dynamic_update_slice(gradient, region + all_grads, corner)
        return (lax.cond(is_live, slot_work, lambda kept: kept, gradient), None)
    start_grad = jnp.zeros(padded.shape, jnp.float32)
    gradient, _ = lax.scan(one_slot, start_grad, jnp.arange(SLOTS, dtype=jnp.int32))
    head_rows = gradient[:, :, :WIN] + gradient[:, :, total_rows:]
    return jnp.concatenate([head_rows, gradient[:, :, WIN:total_rows]], axis=2)
```

```python
import functools
import types

import jax
import jax.numpy as jnp
import numpy as np
from jax import lax
from jax.experimental import pallas as pl
from jax.experimental.pallas import tpu as pltpu
from jax.sharding import PartitionSpec as P

smoothing = 0.25
LEVELS = 32767.0
CHUNKS = 4
MESH = pl.DeviceIdType.MESH


def right_form(matrix):
    return np.block([[matrix.real, matrix.imag], [-matrix.imag, matrix.real]])


def make_tables(length):
    half = length // 2
    index = np.arange(length)
    dft = np.exp(-2j * np.pi * (np.outer(index, index) % length) / length) / np.sqrt(length)
    freq = (index + half) % length - half
    fresnel = np.exp(-1j * np.pi * freq.astype(np.float64) ** 2 / (2.0 * length))
    prop = dft.conj() @ (fresnel[:, None] * dft)
    first, second = prop[:half, :half], prop[:half, half:]
    parts = [(first + second) / 2, (first - second) / 2, dft[:half, 0::2], dft[:half, 1::2]]
    tables = []
    for part in parts:
        right = right_form(part)
        tables += [right, right.T]
    stacked = np.stack(tables).astype(np.float32)
    high = stacked.astype(jnp.bfloat16)
    low = (stacked - high.astype(np.float32)).astype(jnp.bfloat16)
    order = np.concatenate([np.arange(0, length, 2), np.arange(1, length, 2)])
    pick = np.zeros((length, length), np.float32)
    pick[np.arange(length), order] = 1.0
    picks = np.stack([pick, pick.T]).astype(jnp.bfloat16)
    return np.concatenate([high, low, picks], axis=0)


def parts_of(value):
    high = value.astype(jnp.bfloat16)
    low = (value - high.astype(jnp.float32)).astype(jnp.bfloat16)
    return high, low


def dot(a, b):
    return jnp.dot(a, b, preferred_element_type=jnp.float32)


def scratch_list(depth_count, stripe_count, capacity, length, width, tables):
    dma, regular = pltpu.SemaphoreType.DMA, pltpu.SemaphoreType.REGULAR
    chunk = length // CHUNKS
    count = tables // 4
    field = (2, length, length)
    items = [
        ("obj", pltpu.VMEM((2, length, width), jnp.float32)),
        ("stage", pltpu.VMEM((2, length, width), jnp.int16)),
        ("win", pltpu.VMEM((capacity, length, length), jnp.int16)),
        ("wins", pltpu.VMEM((depth_count,) + field, jnp.int16)),
        ("waves", pltpu.VMEM((depth_count,) + field, jnp.float32)),
        ("gout", pltpu.VMEM((depth_count,) + field, jnp.int16)),
        ("gscale", pltpu.VMEM((depth_count, 2, CHUNKS, 1, length), jnp.float32)),
        ("gin", pltpu.VMEM((capacity, length, length), jnp.int16)),
        ("gin_scale", pltpu.VMEM((capacity, CHUNKS, 1, length), jnp.float32)),
        ("rstack", pltpu.VMEM((count, 3 * length, length), jnp.bfloat16)),
        ("lstack", pltpu.VMEM((count, length, 3 * length), jnp.bfloat16)),
        ("picks", pltpu.VMEM((2, length, length), jnp.bfloat16)),
        ("probe", pltpu.VMEM(field, jnp.bfloat16)),
        ("amp", pltpu.VMEM((capacity, length, length), jnp.bfloat16)),
        ("amp_send", pltpu.VMEM((2, length, length), jnp.bfloat16)),
        ("patterns", pltpu.VMEM((stripe_count, length, length), jnp.bfloat16)),
        ("adj", pltpu.VMEM(field, jnp.float32)),
        ("far", pltpu.VMEM((2, length, width), jnp.int16)),
        ("far_scale", pltpu.VMEM((2, CHUNKS, 1, width), jnp.float32)),
        ("given", pltpu.VMEM((2, length, width), jnp.int16)),
        ("given_scale", pltpu.VMEM((2, CHUNKS, 1, width), jnp.float32)),
        ("own", pltpu.VMEM((length, width), jnp.float32)),
        ("mate", pltpu.VMEM((length, width), jnp.float32)),
        ("mate_in", pltpu.VMEM((length, width), jnp.float32)),
        ("out", pltpu.VMEM((2, length, width), jnp.float32)),
        ("sem_obj", dma((CHUNKS,))),
        ("sem_r", dma((count,))),
        ("sem_l", dma((count,))),
        ("sem_p", dma((3,))),
        ("sem_out", dma((CHUNKS,))),
        ("ready", regular((capacity,))),
        ("send_n", dma((3,))),
        ("recv_n", dma((CHUNKS, stripe_count))),
        ("send_w", dma((capacity,))),
        ("recv_w", dma((depth_count,))),
        ("send_a", dma((2,))),
        ("recv_a", dma((stripe_count,))),
        ("send_g", dma((depth_count, 2))),
        ("send_gs", dma((depth_count, 2))),
        ("recv_g", dma((capacity, CHUNKS))),
        ("recv_gs", dma((capacity,))),
        ("send_f", dma((2,))),
        ("send_fs", dma((2,))),
        ("recv_f", dma((2, CHUNKS))),
        ("recv_fs", dma((2, CHUNKS))),
        ("send_m", dma),
        ("recv_m", dma((CHUNKS,))),
    ]
    for k in range(CHUNKS):
        items.append((f"slab{k}", pltpu.VMEM((stripe_count, chunk, width), jnp.int16)))
    return items


def kernel(names, sizes, positions_ref, counts_ref, object_hbm, probe_hbm, amp_hbm, table_hbm, out_hbm, *scratch):
    depth_count, stripe_count, capacity, length, width = sizes
    x = types.SimpleNamespace(**dict(zip(names, scratch, strict=True)))
    slabs = [getattr(x, f"slab{k}") for k in range(CHUNKS)]
    half, chunk = length // 2, length // CHUNKS
    count = x.rstack.shape[0]
    me, stripe = lax.axis_index("depth"), lax.axis_index("stripe")
    core, side = lax.rem(stripe, 2), stripe // 2
    partner = stripe + 1 - 2 * core
    across = lax.rem(2 * side + 2, stripe_count)
    first_worker = depth_count // 2 - capacity // 2
    workers = [first_worker + j for j in range(capacity)]
    in_plane = (me >= first_worker) & (me < first_worker + capacity)
    my_j = jnp.clip(me - first_worker, 0, capacity - 1)
    is_worker = in_plane & (core == 0)
    rows_of = [pl.ds(k * chunk, chunk) for k in range(CHUNKS)]

    def remote(src, dst, send, recv, depth, where):
        return pltpu.make_async_remote_copy(
            src_ref=src, dst_ref=dst, send_sem=send, recv_sem=recv, device_id=(depth, where), device_id_type=MESH
        )

    def arrived(ref, sem):
        pltpu.make_async_copy(ref, ref, sem).wait()

    def slot_of(place):
        owner, passed, start = jnp.int32(0), jnp.int32(0), jnp.int32(0)
        for other in range(1, stripe_count):
            passed = passed + counts_ref[other - 1]
            owner = owner + jnp.where(place >= passed, 1, 0)
            start = jnp.where(place >= passed, passed, start)
        within = jnp.clip(place - start, 0, capacity - 1)
        slot = owner * capacity + within
        return owner, within, positions_ref[0, slot], positions_ref[1, slot]

    for k in range(CHUNKS):
        pltpu.make_async_copy(object_hbm.at[0, :, rows_of[k]], x.obj.at[:, rows_of[k]], x.sem_obj.at[k]).start()

    barrier = pltpu.get_barrier_semaphore()
    for step in range(1, stripe_count):
        other = lax.rem(stripe + step, stripe_count)
        pl.semaphore_signal(barrier, inc=1, device_id=(me, other), device_id_type=MESH)

    @pl.when(is_worker)
    def _():
        @pl.loop(me + 1, depth_count)
        def _(layer):
            for cc in range(2):
                pl.semaphore_signal(barrier, inc=1, device_id=(layer, 2 * side + cc), device_id_type=MESH)

    @pl.when(jnp.logical_not(is_worker))
    def _():
        for worker in workers:
            @pl.when(me < worker)
            def _():
                pl.semaphore_signal(barrier, inc=1, device_id=(worker, 2 * side), device_id_type=MESH)

    @pl.when(in_plane)
    def _():
        pltpu.make_async_copy(amp_hbm, x.amp, x.sem_p.at[0]).start()
        pltpu.make_async_copy(table_hbm.at[pl.ds(4 * count, 2)], x.picks, x.sem_p.at[1]).start()

    @pl.when(is_worker)
    def _():
        pltpu.make_async_copy(probe_hbm, x.probe, x.sem_p.at[2]).start()
        for which in range(count):
            high, low = 2 * which, 2 * count + 2 * which
            for place, source in enumerate((high, low, high)):
                span = pl.ds(place * length, length)
                pltpu.make_async_copy(table_hbm.at[source], x.rstack.at[which, span], x.sem_r.at[which]).start()
                pltpu.make_async_copy(table_hbm.at[source + 1], x.lstack.at[which, :, span], x.sem_l.at[which]).start()

    def quantize(k):
        pltpu.make_async_copy(object_hbm.at[0, :, rows_of[k]], x.obj.at[:, rows_of[k]], x.sem_obj.at[k]).wait()
        for part in range(2):
            whole = jnp.round(x.obj[part, rows_of[k]] * LEVELS).astype(jnp.int32).astype(jnp.int16)
            x.stage[part, rows_of[k]] = whole
        slabs[k][stripe] = x.stage[core, rows_of[k]]

    def spread(k):
        for cc in range(2):
            remote(
                x.stage.at[cc, rows_of[k]], slabs[k].at[stripe], x.send_n.at[cc], x.recv_n.at[k, stripe], me, across + cc
            ).start()
        remote(
            x.stage.at[1 - core, rows_of[k]], slabs[k].at[stripe], x.send_n.at[2], x.recv_n.at[k, stripe], me, partner
        ).start()

    quantize(0)
    with jax.named_scope("barrier"):
        lower_workers = jnp.clip(me - first_worker, 0, capacity)
        pl.semaphore_wait(barrier, stripe_count - 1 + jnp.where(is_worker, 2 * me, lower_workers))

    @pl.when(is_worker)
    def _():
        @pl.loop(0, me)
        def _(layer):
            for cc in range(2):
                pl.semaphore_signal(x.ready.at[my_j], inc=1, device_id=(layer, 2 * side + cc), device_id_type=MESH)

    for k in range(CHUNKS):
        if k > 0:
            quantize(k)
        spread(k)

    @pl.when(in_plane)
    def _():
        pltpu.make_async_copy(amp_hbm, x.amp, x.sem_p.at[0]).wait()
        pltpu.make_async_copy(table_hbm.at[pl.ds(4 * count, 2)], x.picks, x.sem_p.at[1]).wait()
        for target in range(2):
            _, within, _, _ = slot_of(capacity * target + my_j)
            moved = dot(x.picks[0], x.amp[within]).astype(jnp.bfloat16)
            x.amp_send[target] = dot(moved, x.picks[1]).astype(jnp.bfloat16)

            @pl.when(stripe == 2 * target)
            def _():
                pltpu.make_async_copy(x.amp_send.at[target], x.patterns.at[stripe], x.recv_a.at[stripe]).start()

            @pl.when(stripe != 2 * target)
            def _():
                remote(
                    x.amp_send.at[target], x.patterns.at[stripe], x.send_a.at[target], x.recv_a.at[stripe], me, 2 * target
                ).start()

    my_owner, _, my_row, my_col = slot_of(capacity * side + my_j)

    @pl.when(is_worker)
    def _():
        pltpu.make_async_copy(probe_hbm, x.probe, x.sem_p.at[2]).wait()
        first = lax.broadcasted_iota(jnp.int32, (length, length), 0)
        second = lax.broadcasted_iota(jnp.int32, (length, length), 1)
        turned = second + my_row
        turned = jnp.where(turned >= length, turned - length, turned)
        turn_rows = jnp.where(first == turned, 1.0, 0.0).astype(jnp.bfloat16)
        turned = first + my_col
        turned = jnp.where(turned >= length, turned - length, turned)
        turn_cols = jnp.where(second == turned, 1.0, 0.0).astype(jnp.bfloat16)
        for part in range(2):
            value = dot(turn_rows, x.probe[part]).astype(jnp.bfloat16)
            x.waves[0, part] = dot(value, turn_cols)

    row_index = lax.broadcasted_iota(jnp.int32, (chunk, half), 0)
    col_index = lax.broadcasted_iota(jnp.int32, (chunk, half), 1)

    def each_worker(action):
        for j, worker in enumerate(workers):
            here = (me == worker) & (core == 0)
            action(j, worker, here)

    def cut(k):
        for step in range(1, stripe_count):
            other = lax.rem(stripe + step, stripe_count)
            arrived(slabs[k].at[other], x.recv_n.at[k, other])
        for j, worker in enumerate(workers):
            owner, _, row, col = slot_of(capacity * side + j)
            later = lax.rem(owner + 1, stripe_count)
            here = row_index >= row - k * chunk
            near = col_index >= col
            left, mid, right = (
                jnp.where(
                    here,
                    slabs[k][owner, :, pl.ds(place * half, half)].astype(jnp.int32),
                    slabs[k][later, :, pl.ds(place * half, half)].astype(jnp.int32),
                )
                for place in range(3)
            )
            x.win[j, rows_of[k], pl.ds(0, half)] = jnp.where(near, left, right).astype(jnp.int16)
            x.win[j, rows_of[k], pl.ds(half, half)] = mid.astype(jnp.int16)

            local = (me == worker) & (core == 0)
            if k == 0:
                @pl.when(me < worker)
                def _():
                    pl.semaphore_wait(x.ready.at[j], 1)

            source, target = x.win.at[j, rows_of[k]], x.wins.at[me, core, rows_of[k]]

            @pl.when(jnp.logical_not(local))
            def _():
                remote(source, target, x.send_w.at[j], x.recv_w.at[me], worker, 2 * side).start()

            @pl.when(local)
            def _():
                pltpu.make_async_copy(source, target, x.recv_w.at[me]).start()

    for k in range(CHUNKS):
        with jax.named_scope(f"cut{k}"):
            cut(k)

    def right_dot(value, which):
        high, low = parts_of(value)
        return dot(jnp.concatenate([high, high, low], axis=1), x.rstack[which])

    def left_dot(which, value):
        high, low = parts_of(value)
        return dot(x.lstack[which], jnp.concatenate([high, high, low], axis=0))

    def split_lanes(re, im):
        return (
            jnp.concatenate([re[:, :half] + re[:, half:], im[:, :half] + im[:, half:]], axis=1),
            jnp.concatenate([re[:, :half] - re[:, half:], im[:, :half] - im[:, half:]], axis=1),
        )

    def split_rows(re, im):
        return (
            jnp.concatenate([re[:half] + re[half:], im[:half] + im[half:]], axis=0),
            jnp.concatenate([re[:half] - re[half:], im[:half] - im[half:]], axis=0),
        )

    def join_lanes(p, q):
        return (
            jnp.concatenate([p[:, :half] + q[:, :half], p[:, :half] - q[:, :half]], axis=1),
            jnp.concatenate([p[:, half:] + q[:, half:], p[:, half:] - q[:, half:]], axis=1),
        )

    def join_rows(p, q):
        return (
            jnp.concatenate([p[:half] + q[:half], p[:half] - q[:half]], axis=0),
            jnp.concatenate([p[half:] + q[half:], p[half:] - q[half:]], axis=0),
        )

    def propagate(re, im):
        u, v = split_lanes(re, im)
        re, im = join_lanes(right_dot(u, 0), right_dot(v, 1))
        u, v = split_rows(re, im)
        return join_rows(left_dot(0, u), left_dot(1, v))

    def window_of(layer):
        value = x.wins[layer].astype(jnp.int32).astype(jnp.float32) * (1.0 / LEVELS)
        return value[0], value[1]

    def emit(layer, re, im):
        for part, value in enumerate((re, im)):
            for k in range(CHUNKS):
                piece = value[k * chunk : (k + 1) * chunk]
                most = jnp.maximum(jnp.max(jnp.abs(piece), axis=0, keepdims=True), 1e-30)
                x.gout[layer, part, rows_of[k]] = jnp.round(piece * (LEVELS / most)).astype(jnp.int32).astype(jnp.int16)
                x.gscale[layer, part, k] = most * (1.0 / LEVELS)

        def scale_copy(part):
            return remote(
                x.gscale.at[layer, part], x.gin_scale.at[my_j], x.send_gs.at[layer, part], x.recv_gs.at[my_j], layer,
                2 * side + part,
            )

        def chunk_copy(part, k):
            return remote(
                x.gout.at[layer, part, rows_of[k]], x.gin.at[my_j, rows_of[k]], x.send_g.at[layer, part],
                x.recv_g.at[my_j, k], layer, 2 * side + part,
            )

        @pl.when(layer != me)
        def _():
            scale_copy(0).start()

        @pl.when(layer == me)
        def _():
            pltpu.make_async_copy(x.gscale.at[layer, 0], x.gin_scale.at[my_j], x.recv_gs.at[my_j]).start()

        scale_copy(1).start()
        for k in range(CHUNKS):
            @pl.when(layer != me)
            def _():
                chunk_copy(0, k).start()

            @pl.when(layer == me)
            def _():
                pltpu.make_async_copy(
                    x.gout.at[layer, 0, rows_of[k]], x.gin.at[my_j, rows_of[k]], x.recv_g.at[my_j, k]
                ).start()

            chunk_copy(1, k).start()

    @pl.when(is_worker)
    def _():
        for which in range(count):
            arrived(x.rstack.at[which], x.sem_r.at[which])
            arrived(x.lstack.at[which], x.sem_l.at[which])

        @pl.loop(0, depth_count - 1)
        def forward(layer):
            with jax.named_scope("fw_wait"):
                arrived(x.wins.at[layer], x.recv_w.at[layer])
            win_re, win_im = window_of(layer)
            re, im = x.waves[layer, 0], x.waves[layer, 1]
            re, im = propagate(re * win_re - im * win_im, re * win_im + im * win_re)
            x.waves[layer + 1, 0] = re
            x.waves[layer + 1, 1] = im

        last = depth_count - 1
        with jax.named_scope("last_wait"):
            arrived(x.wins.at[last], x.recv_w.at[last])
        win_re, win_im = window_of(last)
        wave_re, wave_im = x.waves[last, 0], x.waves[last, 1]
        re = wave_re * win_re - wave_im * win_im
        im = wave_re * win_im + wave_im * win_re
        u, v = split_lanes(re, im)
        even, odd = right_dot(u, 2), right_dot(v, 3)
        re = jnp.concatenate([even[:, :half], odd[:, :half]], axis=1)
        im = jnp.concatenate([even[:, half:], odd[:, half:]], axis=1)
        u, v = split_rows(re, im)
        even, odd = left_dot(2, u), left_dot(3, v)
        with jax.named_scope("amp_wait"):
            for source in range(stripe_count):
                arrived(x.patterns.at[source], x.recv_a.at[source])
        amp = x.patterns[my_owner].astype(jnp.float32)
        re = jnp.concatenate([even[:half], odd[:half]], axis=0)
        im = jnp.concatenate([even[half:], odd[half:]], axis=0)
        factor = 1.0 - amp / jnp.sqrt(re * re + im * im + smoothing)
        re, im = factor * re, factor * im

        def left_back(which, value):
            high, low = parts_of(value)
            table = x.rstack[which, pl.ds(0, length)]
            table_low = x.rstack[which, pl.ds(length, length)]
            return dot(table, high) + dot(table_low, high) + dot(table, low)

        def right_back(value, which):
            high, low = parts_of(value)
            table = x.lstack[which, :, pl.ds(0, length)]
            table_low = x.lstack[which, :, pl.ds(length, length)]
            return dot(high, table) + dot(high, table_low) + dot(low, table)

        re, im = join_rows(
            left_back(2, jnp.concatenate([re[:half], im[:half]], axis=0)),
            left_back(3, jnp.concatenate([re[half:], im[half:]], axis=0)),
        )
        mid_re, mid_im = join_lanes(
            right_back(jnp.concatenate([re[:, :half], im[:, :half]], axis=1), 2),
            right_back(jnp.concatenate([re[:, half:], im[:, half:]], axis=1), 3),
        )
        emit(
            last,
            wave_re * mid_re + wave_im * mid_im,
            wave_re * mid_im - wave_im * mid_re,
        )
        x.adj[0] = win_re * mid_re + win_im * mid_im
        x.adj[1] = win_im * mid_re - win_re * mid_im

        @pl.loop(1, depth_count)
        def backward(step):
            layer = last - step
            with jax.named_scope("bw"):
                mid_re, mid_conj = propagate(x.adj[0], x.adj[1])
                win_re, win_im = window_of(layer)
                wave_re, wave_im = x.waves[layer, 0], x.waves[layer, 1]
                emit(
                    layer,
                    wave_re * mid_re - wave_im * mid_conj,
                    -(wave_re * mid_conj + wave_im * mid_re),
                )
                x.adj[0] = win_re * mid_re - win_im * mid_conj
                x.adj[1] = win_im * mid_re + win_re * mid_conj

    def far_copy(cc, k):
        return remote(
            x.far.at[cc, rows_of[k]], x.given.at[core, rows_of[k]], x.send_f.at[cc], x.recv_f.at[core, k], me, across + cc
        )

    def far_scale_copy(cc, k):
        return remote(
            x.far_scale.at[cc, k], x.given_scale.at[core, k], x.send_fs.at[cc], x.recv_fs.at[core, k], me, across + cc
        )

    def mate_copy(k):
        return remote(x.mate.at[rows_of[k]], x.mate_in.at[rows_of[k]], x.send_m, x.recv_m.at[k], me, partner)

    def out_copy(k):
        return pltpu.make_async_copy(x.out.at[:, rows_of[k]], out_hbm.at[0, :, rows_of[k]], x.sem_out.at[k])

    def reduce_chunk(k):
        with jax.named_scope(f"gin_wait{k}"):
            for j in range(capacity):
                if k == 0:
                    arrived(x.gin_scale.at[j], x.recv_gs.at[j])
                arrived(x.gin.at[j, rows_of[k]], x.recv_g.at[j, k])
        targets = [stripe, partner, across, across + 1]
        sums = [[0.0] * 3 for _ in targets]
        for j in range(capacity):
            owner, _, row, col = slot_of(capacity * side + j)
            later = lax.rem(owner + 1, stripe_count)
            here = row_index >= row - k * chunk
            near = col_index >= col
            scale = x.gin_scale[j, k]
            left = x.gin[j, rows_of[k], pl.ds(0, half)].astype(jnp.int32).astype(jnp.float32) * scale[:, :half]
            mid = x.gin[j, rows_of[k], pl.ds(half, half)].astype(jnp.int32).astype(jnp.float32) * scale[:, half:]
            pieces = (jnp.where(near, left, 0.0), mid, jnp.where(near, 0.0, left))
            for t, target in enumerate(targets):
                gain = jnp.where(
                    here, jnp.where(owner == target, 1.0, 0.0), jnp.where(later == target, 1.0, 0.0)
                )
                for place, piece in enumerate(pieces):
                    sums[t][place] = sums[t][place] + piece * gain
        for cc in range(2):
            for place in range(3):
                lanes = pl.ds(place * half, half)
                total = sums[2 + cc][place]
                most = jnp.maximum(jnp.max(jnp.abs(total), axis=0, keepdims=True), 1e-30)
                x.far[cc, rows_of[k], lanes] = jnp.round(total * (LEVELS / most)).astype(jnp.int32).astype(jnp.int16)
                x.far_scale[cc, k, :, lanes] = most * (1.0 / LEVELS)
            far_copy(cc, k).start()
            far_scale_copy(cc, k).start()
        for place in range(3):
            lanes = pl.ds(place * half, half)
            x.mate[rows_of[k], lanes] = sums[1][place]
            x.own[rows_of[k], lanes] = sums[0][place]
        mate_copy(k).start()

    def finish_chunk(k):
        with jax.named_scope(f"far_wait{k}"):
            for part in range(2):
                arrived(x.given.at[part, rows_of[k]], x.recv_f.at[part, k])
                arrived(x.given_scale.at[part, k], x.recv_fs.at[part, k])
            arrived(x.mate_in.at[rows_of[k]], x.recv_m.at[k])
        for part, base in ((core, x.own), (1 - core, x.mate_in)):
            value = x.given[part, rows_of[k]].astype(jnp.int32).astype(jnp.float32)
            x.out[part, rows_of[k]] = base[rows_of[k]] + value * x.given_scale[part, k]
        out_copy(k).start()

    for k in range(CHUNKS):
        reduce_chunk(k)
        if k > 0:
            finish_chunk(k - 1)
    finish_chunk(CHUNKS - 1)

    for k in range(CHUNKS):
        out_copy(k).wait()
    for cc in range(2):
        arrived(x.stage.at[cc], x.send_n.at[cc])
        arrived(x.far.at[cc], x.send_f.at[cc])
        arrived(x.far_scale.at[cc], x.send_fs.at[cc])
    arrived(x.stage.at[0], x.send_n.at[2])
    arrived(x.mate, x.send_m)
    for j, worker in enumerate(workers):
        @pl.when(jnp.logical_not((me == worker) & (core == 0)))
        def _():
            arrived(x.win.at[j], x.send_w.at[j])

    @pl.when(in_plane)
    def _():
        for target in range(2):
            @pl.when(stripe != 2 * target)
            def _():
                arrived(x.amp_send.at[target], x.send_a.at[target])

    @pl.when(is_worker)
    def _():
        @pl.loop(0, depth_count)
        def _(layer):
            arrived(x.gout.at[layer, 1], x.send_g.at[layer, 1])
            arrived(x.gscale.at[layer, 1], x.send_gs.at[layer, 1])

            @pl.when(layer != me)
            def _():
                arrived(x.gout.at[layer, 0], x.send_g.at[layer, 0])
                arrived(x.gscale.at[layer, 0], x.send_gs.at[layer, 0])


def body(tables, object_slices, probe_wave, amplitudes, positions, counts):
    stripe_count = lax.axis_size("stripe")
    depth_count = lax.axis_size("depth")
    layers, _, stripe_rows, width = object_slices.shape
    length = probe_wave.shape[1]
    capacity = amplitudes.shape[0]
    assert layers == 1 and stripe_rows == length and 2 * width == 3 * length
    assert depth_count >= capacity and stripe_count == 4
    items = scratch_list(depth_count, stripe_count, capacity, length, width, tables.shape[0] - 2)
    smem = pl.BlockSpec(memory_space=pltpu.SMEM)
    sizes = (depth_count, stripe_count, capacity, length, width)
    return pl.pallas_call(
        functools.partial(kernel, [name for name, _ in items], sizes),
        out_shape=jax.ShapeDtypeStruct(object_slices.shape, jnp.float32),
        in_specs=[smem] * 2 + [pl.BlockSpec(memory_space=pl.ANY)] * 4,
        out_specs=pl.BlockSpec(memory_space=pl.ANY),
        scratch_shapes=[shape for _, shape in items],
        compiler_params=pltpu.CompilerParams(
            collective_id=0, has_side_effects=True, vmem_limit_bytes=60 * 1024 * 1024
        ),
    )(positions.T, counts, object_slices, probe_wave, amplitudes, tables)


def solution(mesh):
    def run(object_slices, probe_wave, amplitudes, positions, counts):
        tables = jnp.asarray(make_tables(probe_wave.shape[1]))
        return jax.shard_map(
            body,
            mesh=mesh,
            in_specs=(P(), P("depth", None, "stripe", None), P(), P("stripe", None, None), P(), P()),
            out_specs=P("depth", None, "stripe", None),
            check_vma=False,
        )(tables, object_slices, probe_wave, amplitudes, positions, counts)

    return run
```

```python
import functools
import types

import jax
import jax.numpy as jnp
import numpy as np
from jax import lax
from jax.experimental import pallas as pl
from jax.experimental.pallas import tpu as pltpu
from jax.sharding import PartitionSpec as P

smoothing = 0.25
LEVELS = 32767.0
IN_CUTS = (32, 64, 80, 80)
OUT_CUTS = (64, 64, 64, 64)
LATE = 4
ORDER = (2, 3, 1, 0)
MESH = pl.DeviceIdType.MESH


def right_form(matrix):
    return np.block([[matrix.real, matrix.imag], [-matrix.imag, matrix.real]])


def make_tables(length):
    half = length // 2
    index = np.arange(length)
    dft = np.exp(-2j * np.pi * (np.outer(index, index) % length) / length) / np.sqrt(length)
    freq = (index + half) % length - half
    fresnel = np.exp(-1j * np.pi * freq.astype(np.float64) ** 2 / (2.0 * length))
    prop = dft.conj() @ (fresnel[:, None] * dft)
    first, second = prop[:half, :half], prop[:half, half:]
    parts = [(first + second) / 2, (first - second) / 2, dft[:half, 0::2], dft[:half, 1::2]]
    tables = []
    for part in parts:
        right = right_form(part)
        tables += [right, right.T]
    stacked = np.stack(tables).astype(np.float32)
    high = stacked.astype(jnp.bfloat16)
    low = (stacked - high.astype(np.float32)).astype(jnp.bfloat16)
    order = np.concatenate([np.arange(0, length, 2), np.arange(1, length, 2)])
    pick = np.zeros((length, length), np.float32)
    pick[np.arange(length), order] = 1.0
    picks = np.stack([pick, pick.T]).astype(jnp.bfloat16)
    return np.concatenate([high, low, picks], axis=0)


def cut_rows(length, cuts):
    unit = length // sum(cuts)
    sizes = [size * unit for size in cuts]
    return [(sum(sizes[:k]), size) for k, size in enumerate(sizes)]


def worker_depths(depth_count):
    return [depth_count // 8, depth_count // 4, depth_count // 2, depth_count // 2 + 1]


def parts_of(value):
    high = value.astype(jnp.bfloat16)
    low = (value - high.astype(jnp.float32)).astype(jnp.bfloat16)
    return high, low


def dot(a, b):
    return jnp.dot(a, b, preferred_element_type=jnp.float32)


def scratch_list(depth_count, stripe_count, capacity, length, width, tables):
    dma, regular = pltpu.SemaphoreType.DMA, pltpu.SemaphoreType.REGULAR
    count = tables // 4
    ins, outs = len(IN_CUTS), len(OUT_CUTS)
    field = (2, length, length)
    items = [
        ("obj", pltpu.VMEM((2, length, width), jnp.float32)),
        ("stage", pltpu.VMEM((2, length, width), jnp.int16)),
        ("win", pltpu.VMEM((capacity, length, length), jnp.int16)),
        ("wins", pltpu.VMEM((depth_count,) + field, jnp.int16)),
        ("waves", pltpu.VMEM((depth_count,) + field, jnp.float32)),
        ("gout", pltpu.VMEM((depth_count,) + field, jnp.int16)),
        ("gscale", pltpu.VMEM((depth_count, 2, outs, 1, length), jnp.float32)),
        ("gin", pltpu.VMEM((capacity, length, length), jnp.int16)),
        ("gin_scale", pltpu.VMEM((capacity, outs, 1, length), jnp.float32)),
        ("rstack", pltpu.VMEM((count, 3 * length, length), jnp.bfloat16)),
        ("lstack", pltpu.VMEM((count, length, 3 * length), jnp.bfloat16)),
        ("picks", pltpu.VMEM((2, length, length), jnp.bfloat16)),
        ("probe", pltpu.VMEM(field, jnp.bfloat16)),
        ("amp", pltpu.VMEM((capacity, length, length), jnp.bfloat16)),
        ("amp_send", pltpu.VMEM((2, length, length), jnp.bfloat16)),
        ("patterns", pltpu.VMEM((stripe_count, length, length), jnp.bfloat16)),
        ("adj", pltpu.VMEM(field, jnp.float32)),
        ("far", pltpu.VMEM((2, length, width), jnp.int16)),
        ("far_scale", pltpu.VMEM((2, outs, 1, width), jnp.float32)),
        ("given", pltpu.VMEM((2, length, width), jnp.int16)),
        ("given_scale", pltpu.VMEM((2, outs, 1, width), jnp.float32)),
        ("own", pltpu.VMEM((length, width), jnp.float32)),
        ("mate", pltpu.VMEM((length, width), jnp.float32)),
        ("mate_in", pltpu.VMEM((length, width), jnp.float32)),
        ("positions", pltpu.SMEM((2, stripe_count * capacity), jnp.int32)),
        ("counts", pltpu.SMEM((stripe_count,), jnp.int32)),
        ("sem_s", dma((2,))),
        ("sem_obj", dma((ins,))),
        ("sem_r", dma((count,))),
        ("sem_l", dma((count,))),
        ("sem_p", dma((3,))),
        ("ready", regular((capacity,))),
        ("send_n", dma((3,))),
        ("recv_n", dma((ins, stripe_count))),
        ("send_w", dma((capacity,))),
        ("recv_w", dma((depth_count,))),
        ("send_a", dma((2,))),
        ("recv_a", dma((stripe_count,))),
        ("send_g", dma((depth_count, 2))),
        ("send_gs", dma((depth_count, 2))),
        ("recv_g", dma((capacity, outs))),
        ("recv_gs", dma((capacity,))),
        ("send_f", dma((2,))),
        ("send_fs", dma((2,))),
        ("recv_f", dma((2, outs))),
        ("recv_fs", dma((2, outs))),
        ("send_m", dma),
        ("recv_m", dma((outs,))),
    ]
    for k, (_, size) in enumerate(cut_rows(length, IN_CUTS)):
        items.append((f"slab{k}", pltpu.VMEM((stripe_count, size, width), jnp.int16)))
    return items


def kernel(names, sizes, positions_hbm, counts_hbm, object_hbm, probe_hbm, amp_hbm, table_hbm, out_ref, *scratch):
    depth_count, stripe_count, capacity, length, width = sizes
    x = types.SimpleNamespace(**dict(zip(names, scratch, strict=True)))
    in_cuts, out_cuts = cut_rows(length, IN_CUTS), cut_rows(length, OUT_CUTS)
    ins, outs = len(in_cuts), len(out_cuts)
    in_rows = [pl.ds(start, size) for start, size in in_cuts]
    out_rows = [pl.ds(start, size) for start, size in out_cuts]
    slabs = [getattr(x, f"slab{k}") for k in range(ins)]
    half = length // 2
    count = x.rstack.shape[0]
    me, stripe = lax.axis_index("depth"), lax.axis_index("stripe")
    core, side = lax.rem(stripe, 2), stripe // 2
    partner = stripe + 1 - 2 * core
    across = lax.rem(2 * side + 2, stripe_count)
    workers = worker_depths(depth_count)
    in_plane = functools.reduce(jnp.logical_or, [me == worker for worker in workers])
    my_j = sum(jnp.where(me == worker, j, 0) for j, worker in enumerate(workers))
    is_worker = in_plane & (core == 0)

    def remote(src, dst, send, recv, depth, where):
        return pltpu.make_async_remote_copy(
            src_ref=src, dst_ref=dst, send_sem=send, recv_sem=recv, device_id=(depth, where), device_id_type=MESH
        )

    def arrived(ref, sem):
        pltpu.make_async_copy(ref, ref, sem).wait()

    def slot_of(place):
        owner, passed, start = jnp.int32(0), jnp.int32(0), jnp.int32(0)
        for other in range(1, stripe_count):
            passed = passed + x.counts[other - 1]
            owner = owner + jnp.where(place >= passed, 1, 0)
            start = jnp.where(place >= passed, passed, start)
        within = jnp.clip(place - start, 0, capacity - 1)
        slot = owner * capacity + within
        return owner, within, x.positions[0, slot], x.positions[1, slot]

    def scalar_loads():
        return [
            pltpu.make_async_copy(positions_hbm, x.positions, x.sem_s.at[0]),
            pltpu.make_async_copy(counts_hbm, x.counts, x.sem_s.at[1]),
        ]

    for k in range(ins):
        pltpu.make_async_copy(object_hbm.at[0, :, in_rows[k]], x.obj.at[:, in_rows[k]], x.sem_obj.at[k]).start()

    for copy in scalar_loads():
        copy.start()

    barrier = pltpu.get_barrier_semaphore()
    for step in range(1, stripe_count):
        other = lax.rem(stripe + step, stripe_count)
        pl.semaphore_signal(barrier, inc=1, device_id=(me, other), device_id_type=MESH)

    @pl.when(is_worker)
    def _():
        @pl.loop(me + 1, depth_count)
        def _(layer):
            for cc in range(2):
                pl.semaphore_signal(barrier, inc=1, device_id=(layer, 2 * side + cc), device_id_type=MESH)

    @pl.when(jnp.logical_not(is_worker))
    def _():
        for worker in workers:
            @pl.when(me < worker)
            def _():
                pl.semaphore_signal(barrier, inc=1, device_id=(worker, 2 * side), device_id_type=MESH)

    @pl.when(in_plane)
    def _():
        pltpu.make_async_copy(amp_hbm, x.amp, x.sem_p.at[0]).start()
        pltpu.make_async_copy(table_hbm.at[pl.ds(4 * count, 2)], x.picks, x.sem_p.at[1]).start()

    @pl.when(is_worker)
    def _():
        pltpu.make_async_copy(probe_hbm, x.probe, x.sem_p.at[2]).start()
        for which in range(count):
            high, low = 2 * which, 2 * count + 2 * which
            for place, source in enumerate((high, low, high)):
                span = pl.ds(place * length, length)
                pltpu.make_async_copy(table_hbm.at[source], x.rstack.at[which, span], x.sem_r.at[which]).start()
                pltpu.make_async_copy(table_hbm.at[source + 1], x.lstack.at[which, :, span], x.sem_l.at[which]).start()

    def quantize(k):
        pltpu.make_async_copy(object_hbm.at[0, :, in_rows[k]], x.obj.at[:, in_rows[k]], x.sem_obj.at[k]).wait()
        for part in range(2):
            whole = jnp.round(x.obj[part, in_rows[k]] * LEVELS).astype(jnp.int32).astype(jnp.int16)
            x.stage[part, in_rows[k]] = whole
        slabs[k][stripe] = x.stage[core, in_rows[k]]

    def spread(k):
        for cc in range(2):
            remote(
                x.stage.at[cc, in_rows[k]], slabs[k].at[stripe], x.send_n.at[cc], x.recv_n.at[k, stripe], me, across + cc
            ).start()
        remote(
            x.stage.at[1 - core, in_rows[k]], slabs[k].at[stripe], x.send_n.at[2], x.recv_n.at[k, stripe], me, partner
        ).start()

    quantize(0)
    with jax.named_scope("barrier"):
        lower_workers = sum(jnp.where(worker < me, 1, 0) for worker in workers)
        pl.semaphore_wait(barrier, stripe_count - 1 + jnp.where(is_worker, 2 * me, lower_workers))

    @pl.when(is_worker)
    def _():
        @pl.loop(0, me)
        def _(layer):
            for cc in range(2):
                pl.semaphore_signal(x.ready.at[my_j], inc=1, device_id=(layer, 2 * side + cc), device_id_type=MESH)

    for k in range(ins):
        if k > 0:
            quantize(k)
        spread(k)

    for copy in scalar_loads():
        copy.wait()

    @pl.when(in_plane)
    def _():
        pltpu.make_async_copy(amp_hbm, x.amp, x.sem_p.at[0]).wait()
        pltpu.make_async_copy(table_hbm.at[pl.ds(4 * count, 2)], x.picks, x.sem_p.at[1]).wait()
        for target in range(2):
            _, within, _, _ = slot_of(capacity * target + my_j)
            moved = dot(x.picks[0], x.amp[within]).astype(jnp.bfloat16)
            x.amp_send[target] = dot(moved, x.picks[1]).astype(jnp.bfloat16)

            @pl.when(stripe == 2 * target)
            def _():
                pltpu.make_async_copy(x.amp_send.at[target], x.patterns.at[stripe], x.recv_a.at[stripe]).start()

            @pl.when(stripe != 2 * target)
            def _():
                remote(
                    x.amp_send.at[target], x.patterns.at[stripe], x.send_a.at[target], x.recv_a.at[stripe], me, 2 * target
                ).start()

    my_owner, _, my_row, my_col = slot_of(capacity * side + my_j)

    @pl.when(is_worker)
    def _():
        pltpu.make_async_copy(probe_hbm, x.probe, x.sem_p.at[2]).wait()
        first = lax.broadcasted_iota(jnp.int32, (length, length), 0)
        second = lax.broadcasted_iota(jnp.int32, (length, length), 1)
        turned = second + my_row
        turned = jnp.where(turned >= length, turned - length, turned)
        turn_rows = jnp.where(first == turned, 1.0, 0.0).astype(jnp.bfloat16)
        turned = first + my_col
        turned = jnp.where(turned >= length, turned - length, turned)
        turn_cols = jnp.where(second == turned, 1.0, 0.0).astype(jnp.bfloat16)
        for part in range(2):
            value = dot(turn_rows, x.probe[part]).astype(jnp.bfloat16)
            x.waves[0, part] = dot(value, turn_cols)

    def rows_from(size):
        return lax.broadcasted_iota(jnp.int32, (size, half), 0)

    def cols_from(size):
        return lax.broadcasted_iota(jnp.int32, (size, half), 1)

    order = ORDER

    def local(j):
        return (me == workers[j]) & (core == 0)

    def window_send(j, rows):
        source, target = x.win.at[j, rows], x.wins.at[me, core, rows]

        @pl.when(jnp.logical_not(local(j)))
        def _():
            remote(source, target, x.send_w.at[j], x.recv_w.at[me], workers[j], 2 * side).start()

        @pl.when(local(j))
        def _():
            pltpu.make_async_copy(source, target, x.recv_w.at[me]).start()

    def cut(k):
        for step in range(1, stripe_count):
            other = lax.rem(stripe + step, stripe_count)
            arrived(slabs[k].at[other], x.recv_n.at[k, other])
        start, size = in_cuts[k]
        for j in order:
            owner, _, row, col = slot_of(capacity * side + j)
            later = lax.rem(owner + 1, stripe_count)
            here = rows_from(size) >= row - start
            near = cols_from(size) >= col
            left, mid, right = (
                jnp.where(
                    here,
                    slabs[k][owner, :, pl.ds(place * half, half)].astype(jnp.int32),
                    slabs[k][later, :, pl.ds(place * half, half)].astype(jnp.int32),
                )
                for place in range(3)
            )
            x.win[j, in_rows[k], pl.ds(0, half)] = jnp.where(near, left, right).astype(jnp.int16)
            x.win[j, in_rows[k], pl.ds(half, half)] = mid.astype(jnp.int16)

            if k == 0:
                @pl.when(me < workers[j])
                def _():
                    pl.semaphore_wait(x.ready.at[j], 1)

    for k in range(ins):
        with jax.named_scope(f"cut{k}"):
            cut(k)
        for j in order:
            window_send(j, in_rows[k])

    def right_dot(value, which):
        high, low = parts_of(value)
        return dot(jnp.concatenate([high, high, low], axis=1), x.rstack[which])

    def left_dot(which, value):
        high, low = parts_of(value)
        return dot(x.lstack[which], jnp.concatenate([high, high, low], axis=0))

    def split_lanes(re, im):
        return (
            jnp.concatenate([re[:, :half] + re[:, half:], im[:, :half] + im[:, half:]], axis=1),
            jnp.concatenate([re[:, :half] - re[:, half:], im[:, :half] - im[:, half:]], axis=1),
        )

    def split_rows(re, im):
        return (
            jnp.concatenate([re[:half] + re[half:], im[:half] + im[half:]], axis=0),
            jnp.concatenate([re[:half] - re[half:], im[:half] - im[half:]], axis=0),
        )

    def join_lanes(p, q):
        return (
            jnp.concatenate([p[:, :half] + q[:, :half], p[:, :half] - q[:, :half]], axis=1),
            jnp.concatenate([p[:, half:] + q[:, half:], p[:, half:] - q[:, half:]], axis=1),
        )

    def join_rows(p, q):
        return (
            jnp.concatenate([p[:half] + q[:half], p[:half] - q[:half]], axis=0),
            jnp.concatenate([p[half:] + q[half:], p[half:] - q[half:]], axis=0),
        )

    def propagate(re, im):
        u, v = split_lanes(re, im)
        re, im = join_lanes(right_dot(u, 0), right_dot(v, 1))
        u, v = split_rows(re, im)
        return join_rows(left_dot(0, u), left_dot(1, v))

    def window_of(layer):
        value = x.wins[layer].astype(jnp.int32).astype(jnp.float32) * (1.0 / LEVELS)
        return value[0], value[1]

    def gradient_copies(layer, k, action):
        for part in range(2):
            @pl.when((layer != me) | (part == 1))
            def _():
                action(
                    remote(
                        x.gout.at[layer, part, out_rows[k]], x.gin.at[my_j, out_rows[k]], x.send_g.at[layer, part],
                        x.recv_g.at[my_j, k], layer, 2 * side + part,
                    )
                )

        @pl.when(layer == me)
        def _():
            action(
                pltpu.make_async_copy(
                    x.gout.at[layer, 0, out_rows[k]], x.gin.at[my_j, out_rows[k]], x.recv_g.at[my_j, k]
                )
            )

    def emit(layer, re, im):
        for part, value in enumerate((re, im)):
            for k in range(outs):
                start, size = out_cuts[k]
                piece = value[start : start + size]
                most = jnp.maximum(jnp.max(jnp.abs(piece), axis=0, keepdims=True), 1e-30)
                x.gout[layer, part, out_rows[k]] = jnp.round(piece * (LEVELS / most)).astype(jnp.int32).astype(jnp.int16)
                x.gscale[layer, part, k] = most * (1.0 / LEVELS)

        def scale_copy(part):
            return remote(
                x.gscale.at[layer, part], x.gin_scale.at[my_j], x.send_gs.at[layer, part], x.recv_gs.at[my_j], layer,
                2 * side + part,
            )

        @pl.when(layer != me)
        def _():
            scale_copy(0).start()

        @pl.when(layer == me)
        def _():
            pltpu.make_async_copy(x.gscale.at[layer, 0], x.gin_scale.at[my_j], x.recv_gs.at[my_j]).start()

        scale_copy(1).start()
        for k in range(outs):
            held = layer + k

            @pl.when((held < depth_count) & ((held >= LATE) | (k == 0)))
            def _():
                gradient_copies(held, k, lambda copy: copy.start())

    @pl.when(is_worker)
    def _():
        for which in range(count):
            arrived(x.rstack.at[which], x.sem_r.at[which])
            arrived(x.lstack.at[which], x.sem_l.at[which])

        @pl.loop(0, depth_count - 1)
        def forward(layer):
            with jax.named_scope("fw_wait"):
                arrived(x.wins.at[layer], x.recv_w.at[layer])
            win_re, win_im = window_of(layer)
            re, im = x.waves[layer, 0], x.waves[layer, 1]
            re, im = propagate(re * win_re - im * win_im, re * win_im + im * win_re)
            x.waves[layer + 1, 0] = re
            x.waves[layer + 1, 1] = im

        last = depth_count - 1
        with jax.named_scope("last_wait"):
            arrived(x.wins.at[last], x.recv_w.at[last])
        win_re, win_im = window_of(last)
        wave_re, wave_im = x.waves[last, 0], x.waves[last, 1]
        re = wave_re * win_re - wave_im * win_im
        im = wave_re * win_im + wave_im * win_re
        u, v = split_lanes(re, im)
        even, odd = right_dot(u, 2), right_dot(v, 3)
        re = jnp.concatenate([even[:, :half], odd[:, :half]], axis=1)
        im = jnp.concatenate([even[:, half:], odd[:, half:]], axis=1)
        u, v = split_rows(re, im)
        even, odd = left_dot(2, u), left_dot(3, v)
        with jax.named_scope("amp_wait"):
            for source in range(stripe_count):
                arrived(x.patterns.at[source], x.recv_a.at[source])
        amp = x.patterns[my_owner].astype(jnp.float32)
        re = jnp.concatenate([even[:half], odd[:half]], axis=0)
        im = jnp.concatenate([even[half:], odd[half:]], axis=0)
        factor = 1.0 - amp / jnp.sqrt(re * re + im * im + smoothing)
        re, im = factor * re, factor * im

        def left_back(which, value):
            high, low = parts_of(value)
            table = x.rstack[which, pl.ds(0, length)]
            table_low = x.rstack[which, pl.ds(length, length)]
            return dot(table, high) + dot(table_low, high) + dot(table, low)

        def right_back(value, which):
            high, low = parts_of(value)
            table = x.lstack[which, :, pl.ds(0, length)]
            table_low = x.lstack[which, :, pl.ds(length, length)]
            return dot(high, table) + dot(high, table_low) + dot(low, table)

        re, im = join_rows(
            left_back(2, jnp.concatenate([re[:half], im[:half]], axis=0)),
            left_back(3, jnp.concatenate([re[half:], im[half:]], axis=0)),
        )
        mid_re, mid_im = join_lanes(
            right_back(jnp.concatenate([re[:, :half], im[:, :half]], axis=1), 2),
            right_back(jnp.concatenate([re[:, half:], im[:, half:]], axis=1), 3),
        )
        emit(
            last,
            wave_re * mid_re + wave_im * mid_im,
            wave_re * mid_im - wave_im * mid_re,
        )
        x.adj[0] = win_re * mid_re + win_im * mid_im
        x.adj[1] = win_im * mid_re - win_re * mid_im

        @pl.loop(1, depth_count)
        def backward(step):
            layer = last - step
            with jax.named_scope("bw"):
                mid_re, mid_conj = propagate(x.adj[0], x.adj[1])
                win_re, win_im = window_of(layer)
                wave_re, wave_im = x.waves[layer, 0], x.waves[layer, 1]
                emit(
                    layer,
                    wave_re * mid_re - wave_im * mid_conj,
                    -(wave_re * mid_conj + wave_im * mid_re),
                )
                x.adj[0] = win_re * mid_re - win_im * mid_conj
                x.adj[1] = win_im * mid_re + win_re * mid_conj

        for k in range(1, outs):
            for layer in range(LATE):
                gradient_copies(layer, k, lambda copy: copy.start())

    def far_copy(cc, k):
        return remote(
            x.far.at[cc, out_rows[k]], x.given.at[core, out_rows[k]], x.send_f.at[cc], x.recv_f.at[core, k], me, across + cc
        )

    def far_scale_copy(cc, k):
        return remote(
            x.far_scale.at[cc, k], x.given_scale.at[core, k], x.send_fs.at[cc], x.recv_fs.at[core, k], me, across + cc
        )

    def mate_copy(k):
        return remote(x.mate.at[out_rows[k]], x.mate_in.at[out_rows[k]], x.send_m, x.recv_m.at[k], me, partner)

    def reduce_chunk(k):
        with jax.named_scope(f"gin_wait{k}"):
            for j in range(capacity):
                if k == 0:
                    arrived(x.gin_scale.at[j], x.recv_gs.at[j])
                arrived(x.gin.at[j, out_rows[k]], x.recv_g.at[j, k])
        start, size = out_cuts[k]
        targets = [stripe, partner, across, across + 1]
        sums = [[0.0] * 3 for _ in targets]
        for j in range(capacity):
            owner, _, row, col = slot_of(capacity * side + j)
            later = lax.rem(owner + 1, stripe_count)
            here = rows_from(size) >= row - start
            near = cols_from(size) >= col
            scale = x.gin_scale[j, k]
            left = x.gin[j, out_rows[k], pl.ds(0, half)].astype(jnp.int32).astype(jnp.float32) * scale[:, :half]
            mid = x.gin[j, out_rows[k], pl.ds(half, half)].astype(jnp.int32).astype(jnp.float32) * scale[:, half:]
            pieces = (jnp.where(near, left, 0.0), mid, jnp.where(near, 0.0, left))
            for t, target in enumerate(targets):
                gain = jnp.where(
                    here, jnp.where(owner == target, 1.0, 0.0), jnp.where(later == target, 1.0, 0.0)
                )
                for place, piece in enumerate(pieces):
                    sums[t][place] = sums[t][place] + piece * gain
        for cc in range(2):
            for place in range(3):
                lanes = pl.ds(place * half, half)
                total = sums[2 + cc][place]
                most = jnp.maximum(jnp.max(jnp.abs(total), axis=0, keepdims=True), 1e-30)
                x.far[cc, out_rows[k], lanes] = jnp.round(total * (LEVELS / most)).astype(jnp.int32).astype(jnp.int16)
                x.far_scale[cc, k, :, lanes] = most * (1.0 / LEVELS)
            far_copy(cc, k).start()
            far_scale_copy(cc, k).start()
        for place in range(3):
            lanes = pl.ds(place * half, half)
            x.mate[out_rows[k], lanes] = sums[1][place]
            x.own[out_rows[k], lanes] = sums[0][place]
        mate_copy(k).start()

    def finish_chunk(k):
        with jax.named_scope(f"far_wait{k}"):
            for part in range(2):
                arrived(x.given.at[part, out_rows[k]], x.recv_f.at[part, k])
                arrived(x.given_scale.at[part, k], x.recv_fs.at[part, k])
            arrived(x.mate_in.at[out_rows[k]], x.recv_m.at[k])
        for part, base in ((core, x.own), (1 - core, x.mate_in)):
            value = x.given[part, out_rows[k]].astype(jnp.int32).astype(jnp.float32)
            out_ref[0, part, out_rows[k]] = base[out_rows[k]] + value * x.given_scale[part, k]

    for k in range(outs):
        reduce_chunk(k)
        if k > 0:
            finish_chunk(k - 1)
    finish_chunk(outs - 1)

    for cc in range(2):
        arrived(x.stage.at[cc], x.send_n.at[cc])
        arrived(x.far.at[cc], x.send_f.at[cc])
        arrived(x.far_scale.at[cc], x.send_fs.at[cc])
    arrived(x.stage.at[0], x.send_n.at[2])
    arrived(x.mate, x.send_m)
    for j, worker in enumerate(workers):
        @pl.when(jnp.logical_not((me == worker) & (core == 0)))
        def _():
            arrived(x.win.at[j], x.send_w.at[j])

    @pl.when(in_plane)
    def _():
        for target in range(2):
            @pl.when(stripe != 2 * target)
            def _():
                arrived(x.amp_send.at[target], x.send_a.at[target])

    @pl.when(is_worker)
    def _():
        @pl.loop(0, depth_count)
        def _(layer):
            arrived(x.gout.at[layer, 1], x.send_g.at[layer, 1])
            arrived(x.gscale.at[layer, 1], x.send_gs.at[layer, 1])

            @pl.when(layer != me)
            def _():
                arrived(x.gout.at[layer, 0], x.send_g.at[layer, 0])
                arrived(x.gscale.at[layer, 0], x.send_gs.at[layer, 0])


def body(tables, object_slices, probe_wave, amplitudes, positions, counts):
    stripe_count = lax.axis_size("stripe")
    depth_count = lax.axis_size("depth")
    layers, _, stripe_rows, width = object_slices.shape
    length = probe_wave.shape[1]
    capacity = amplitudes.shape[0]
    assert layers == 1 and stripe_rows == length and 2 * width == 3 * length
    assert depth_count % 8 == 0 and stripe_count == 4 and capacity == 4
    items = scratch_list(depth_count, stripe_count, capacity, length, width, tables.shape[0] - 2)
    sizes = (depth_count, stripe_count, capacity, length, width)
    held = sum(
        int(np.prod(shape.shape)) * jnp.dtype(shape.dtype).itemsize
        for _, shape in items
        if getattr(shape, "memory_space", None) == pltpu.VMEM
    )
    operands = (positions.T, counts, object_slices, probe_wave, amplitudes, tables)
    return pl.pallas_call(
        functools.partial(kernel, [name for name, _ in items], sizes),
        out_shape=pltpu.VMEM(object_slices.shape, jnp.float32),
        in_specs=[pl.BlockSpec(memory_space=pl.ANY)] * len(operands),
        out_specs=pl.BlockSpec(memory_space=pltpu.VMEM),
        scratch_shapes=[shape for _, shape in items],
        compiler_params=pltpu.CompilerParams(
            collective_id=0, has_side_effects=True, vmem_limit_bytes=held + (6 << 20)
        ),
    )(*(pltpu.with_memory_space_constraint(operand, pltpu.HBM) for operand in operands))


def solution(mesh):
    def run(object_slices, probe_wave, amplitudes, positions, counts):
        tables = jnp.asarray(make_tables(probe_wave.shape[1]))
        return jax.shard_map(
            body,
            mesh=mesh,
            in_specs=(P(), P("depth", None, "stripe", None), P(), P("stripe", None, None), P(), P()),
            out_specs=P("depth", None, "stripe", None),
            check_vma=False,
        )(tables, object_slices, probe_wave, amplitudes, positions, counts)

    return run
```

```python
import functools
import types

import jax
import jax.numpy as jnp
import numpy as np
from jax import lax
from jax.experimental import pallas as pl
from jax.experimental.pallas import tpu as pltpu
from jax.sharding import PartitionSpec as P

smoothing = 0.25
LEVELS = 32767.0
IN_CUTS = (32, 64, 80, 80)
OUT_CUTS = (64, 64, 64, 64)
LATE = 6
ORDER = (2, 3, 1, 0)
UPPER_LAG = 0
MIDDLE_LAG = 1
MESH = pl.DeviceIdType.MESH


def right_form(matrix):
    return np.block([[matrix.real, matrix.imag], [-matrix.imag, matrix.real]])


def make_tables(length):
    half = length // 2
    index = np.arange(length)
    dft = np.exp(-2j * np.pi * (np.outer(index, index) % length) / length) / np.sqrt(length)
    freq = (index + half) % length - half
    fresnel = np.exp(-1j * np.pi * freq.astype(np.float64) ** 2 / (2.0 * length))
    prop = dft.conj() @ (fresnel[:, None] * dft)
    first, second = prop[:half, :half], prop[:half, half:]
    parts = [(first + second) / 2, (first - second) / 2, dft[:half, 0::2], dft[:half, 1::2]]
    tables = []
    for place, part in enumerate(parts):
        right = right_form(part)
        tables += [right / LEVELS if place < 2 else right, right.T]
    stacked = np.stack(tables).astype(np.float32)
    high = stacked.astype(jnp.bfloat16)
    low = (stacked - high.astype(np.float32)).astype(jnp.bfloat16)
    order = np.concatenate([np.arange(0, length, 2), np.arange(1, length, 2)])
    pick = np.zeros((length, length), np.float32)
    pick[np.arange(length), order] = 1.0
    picks = np.stack([pick, pick.T]).astype(jnp.bfloat16)
    return np.concatenate([high, low, picks], axis=0)


def cut_rows(length, cuts):
    unit = length // sum(cuts)
    sizes = [size * unit for size in cuts]
    return [(sum(sizes[:k]), size) for k, size in enumerate(sizes)]


def worker_depths(depth_count):
    return [depth_count // 8, depth_count // 4, depth_count // 2, depth_count // 2 + 1]


def parts_of(value):
    high = value.astype(jnp.bfloat16)
    low = (value - high.astype(jnp.float32)).astype(jnp.bfloat16)
    return high, low


def dot(a, b):
    return jnp.dot(a, b, preferred_element_type=jnp.float32)


def scratch_list(depth_count, stripe_count, capacity, length, width, tables):
    dma, regular = pltpu.SemaphoreType.DMA, pltpu.SemaphoreType.REGULAR
    count = tables // 4
    ins, outs = len(IN_CUTS), len(OUT_CUTS)
    field = (2, length, length)
    items = [
        ("obj", pltpu.VMEM((2, length, width), jnp.float32)),
        ("stage", pltpu.VMEM((2, length, width), jnp.int16)),
        ("win", pltpu.VMEM((capacity, length, length), jnp.int16)),
        ("wins", pltpu.VMEM((depth_count,) + field, jnp.int16)),
        ("waves", pltpu.VMEM((depth_count,) + field, jnp.float32)),
        ("gout", pltpu.VMEM((2 * depth_count, length, length), jnp.int16)),
        ("gscale", pltpu.VMEM((2 * depth_count, outs, 1, length), jnp.float32)),
        ("gin", pltpu.VMEM((capacity, length, length), jnp.int16)),
        ("gin_scale", pltpu.VMEM((capacity, outs, 1, length), jnp.float32)),
        ("rstack", pltpu.VMEM((count, 3 * length, length), jnp.bfloat16)),
        ("lstack", pltpu.VMEM((count, length, 3 * length), jnp.bfloat16)),
        ("picks", pltpu.VMEM((2, length, length), jnp.bfloat16)),
        ("probe", pltpu.VMEM(field, jnp.bfloat16)),
        ("amp", pltpu.VMEM((capacity, length, length), jnp.bfloat16)),
        ("amp_send", pltpu.VMEM((2, length, length), jnp.bfloat16)),
        ("patterns", pltpu.VMEM((stripe_count, length, length), jnp.bfloat16)),
        ("adj", pltpu.VMEM(field, jnp.float32)),
        ("far", pltpu.VMEM((2, length, width), jnp.int16)),
        ("far_scale", pltpu.VMEM((2, outs, 1, width), jnp.float32)),
        ("given", pltpu.VMEM((2, length, width), jnp.int16)),
        ("given_scale", pltpu.VMEM((2, outs, 1, width), jnp.float32)),
        ("own", pltpu.VMEM((length, width), jnp.float32)),
        ("mate", pltpu.VMEM((length, width), jnp.float32)),
        ("mate_in", pltpu.VMEM((length, width), jnp.float32)),
        ("positions", pltpu.SMEM((2, stripe_count * capacity), jnp.int32)),
        ("counts", pltpu.SMEM((stripe_count,), jnp.int32)),
        ("sem_s", dma((2,))),
        ("sem_obj", dma((ins,))),
        ("sem_r", dma),
        ("sem_l", dma),
        ("sem_p", dma((3,))),
        ("ready", regular((capacity,))),
        ("send_n", dma((2,))),
        ("recv_n", dma((ins,))),
        ("send_w", dma),
        ("recv_w", dma((depth_count,))),
        ("send_a", dma((2,))),
        ("recv_a", dma),
        ("send_g", dma),
        ("send_gs", dma),
        ("recv_g", dma((outs,))),
        ("recv_gs", dma),
        ("send_f", dma),
        ("send_fs", dma),
        ("recv_f", dma((outs,))),
        ("recv_fs", dma((outs,))),
        ("send_m", dma),
        ("recv_m", dma((outs,))),
    ]
    for k, (_, size) in enumerate(cut_rows(length, IN_CUTS)):
        items.append((f"slab{k}", pltpu.VMEM((stripe_count, size, width), jnp.int16)))
    return items


def kernel(names, sizes, positions_hbm, counts_hbm, object_hbm, probe_hbm, amp_hbm, table_hbm, out_ref, *scratch):
    depth_count, stripe_count, capacity, length, width = sizes
    x = types.SimpleNamespace(**dict(zip(names, scratch, strict=True)))
    in_cuts, out_cuts = cut_rows(length, IN_CUTS), cut_rows(length, OUT_CUTS)
    ins, outs = len(in_cuts), len(out_cuts)
    in_rows = [pl.ds(start, size) for start, size in in_cuts]
    out_rows = [pl.ds(start, size) for start, size in out_cuts]
    slabs = [getattr(x, f"slab{k}") for k in range(ins)]
    half = length // 2
    count = x.rstack.shape[0]
    me, stripe = lax.axis_index("depth"), lax.axis_index("stripe")
    core, side = lax.rem(stripe, 2), stripe // 2
    partner = stripe + 1 - 2 * core
    across = lax.rem(2 * side + 2, stripe_count)
    workers = worker_depths(depth_count)
    in_plane = functools.reduce(jnp.logical_or, [me == worker for worker in workers])
    my_j = sum(jnp.where(me == worker, j, 0) for j, worker in enumerate(workers))
    is_worker = in_plane & (core == 0)

    def remote(src, dst, send, recv, depth, where):
        return pltpu.make_async_remote_copy(
            src_ref=src, dst_ref=dst, send_sem=send, recv_sem=recv, device_id=(depth, where), device_id_type=MESH
        )

    def arrived(ref, sem):
        pltpu.make_async_copy(ref, ref, sem).wait()

    def slot_of(place):
        owner, passed, start = jnp.int32(0), jnp.int32(0), jnp.int32(0)
        for other in range(1, stripe_count):
            passed = passed + x.counts[other - 1]
            owner = owner + jnp.where(place >= passed, 1, 0)
            start = jnp.where(place >= passed, passed, start)
        within = jnp.clip(place - start, 0, capacity - 1)
        slot = owner * capacity + within
        return owner, within, x.positions[0, slot], x.positions[1, slot]

    def scalar_loads():
        return [
            pltpu.make_async_copy(positions_hbm, x.positions, x.sem_s.at[0]),
            pltpu.make_async_copy(counts_hbm, x.counts, x.sem_s.at[1]),
        ]

    for k in range(ins):
        pltpu.make_async_copy(object_hbm.at[0, :, in_rows[k]], x.obj.at[:, in_rows[k]], x.sem_obj.at[k]).start()

    for copy in scalar_loads():
        copy.start()

    barrier = pltpu.get_barrier_semaphore()
    for step in range(1, stripe_count):
        other = lax.rem(stripe + step, stripe_count)
        pl.semaphore_signal(barrier, inc=1, device_id=(me, other), device_id_type=MESH)

    @pl.when(is_worker)
    def _():
        @pl.loop(me + 1, depth_count)
        def _(layer):
            for cc in range(2):
                pl.semaphore_signal(barrier, inc=1, device_id=(layer, 2 * side + cc), device_id_type=MESH)

    @pl.when(jnp.logical_not(is_worker))
    def _():
        for worker in workers:
            @pl.when(me < worker)
            def _():
                pl.semaphore_signal(barrier, inc=1, device_id=(worker, 2 * side), device_id_type=MESH)

    @pl.when(in_plane)
    def _():
        pltpu.make_async_copy(amp_hbm, x.amp, x.sem_p.at[0]).start()
        pltpu.make_async_copy(table_hbm.at[pl.ds(4 * count, 2)], x.picks, x.sem_p.at[1]).start()

    @pl.when(is_worker)
    def _():
        pltpu.make_async_copy(probe_hbm, x.probe, x.sem_p.at[2]).start()
        for which in range(count):
            high, low = 2 * which, 2 * count + 2 * which
            for place, source in enumerate((high, low, high)):
                span = pl.ds(place * length, length)
                pltpu.make_async_copy(table_hbm.at[source], x.rstack.at[which, span], x.sem_r).start()
                pltpu.make_async_copy(table_hbm.at[source + 1], x.lstack.at[which, :, span], x.sem_l).start()

    def quantize(k):
        pltpu.make_async_copy(object_hbm.at[0, :, in_rows[k]], x.obj.at[:, in_rows[k]], x.sem_obj.at[k]).wait()
        for part in range(2):
            whole = jnp.round(x.obj[part, in_rows[k]] * LEVELS).astype(jnp.int32).astype(jnp.int16)
            x.stage[part, in_rows[k]] = whole
        slabs[k][stripe] = x.stage[core, in_rows[k]]

    def spread(k):
        for cc in range(2):
            remote(
                x.stage.at[cc, in_rows[k]], slabs[k].at[stripe], x.send_n.at[0], x.recv_n.at[k], me, across + cc
            ).start()
        remote(
            x.stage.at[1 - core, in_rows[k]], slabs[k].at[stripe], x.send_n.at[1], x.recv_n.at[k], me, partner
        ).start()

    quantize(0)
    with jax.named_scope("barrier"):
        lower_workers = sum(jnp.where(worker < me, 1, 0) for worker in workers)
        pl.semaphore_wait(barrier, stripe_count - 1 + jnp.where(is_worker, 2 * me, lower_workers))

    @pl.when(is_worker)
    def _():
        @pl.loop(0, me)
        def _(layer):
            for cc in range(2):
                pl.semaphore_signal(x.ready.at[my_j], inc=1, device_id=(layer, 2 * side + cc), device_id_type=MESH)

    for k in range(ins):
        if k > 0:
            quantize(k)
        spread(k)

    for copy in scalar_loads():
        copy.wait()

    @pl.when(in_plane)
    def _():
        pltpu.make_async_copy(amp_hbm, x.amp, x.sem_p.at[0]).wait()
        pltpu.make_async_copy(table_hbm.at[pl.ds(4 * count, 2)], x.picks, x.sem_p.at[1]).wait()
        for target in range(2):
            _, within, _, _ = slot_of(capacity * target + my_j)
            moved = dot(x.picks[0], x.amp[within]).astype(jnp.bfloat16)
            x.amp_send[target] = dot(moved, x.picks[1]).astype(jnp.bfloat16)

    my_owner, _, my_row, my_col = slot_of(capacity * side + my_j)

    @pl.when(is_worker)
    def _():
        pltpu.make_async_copy(probe_hbm, x.probe, x.sem_p.at[2]).wait()
        first = lax.broadcasted_iota(jnp.int32, (length, length), 0)
        second = lax.broadcasted_iota(jnp.int32, (length, length), 1)
        turned = second + my_row
        turned = jnp.where(turned >= length, turned - length, turned)
        turn_rows = jnp.where(first == turned, 1.0, 0.0).astype(jnp.bfloat16)
        turned = first + my_col
        turned = jnp.where(turned >= length, turned - length, turned)
        turn_cols = jnp.where(second == turned, 1.0, 0.0).astype(jnp.bfloat16)
        for part in range(2):
            value = dot(turn_rows, x.probe[part]).astype(jnp.bfloat16)
            x.waves[0, part] = dot(value, turn_cols)

    def rows_from(size):
        return lax.broadcasted_iota(jnp.int32, (size, half), 0)

    def cols_from(size):
        return lax.broadcasted_iota(jnp.int32, (size, half), 1)

    order = ORDER

    def local(j):
        return (me == workers[j]) & (core == 0)

    def window_send(j, rows):
        source, target = x.win.at[j, rows], x.wins.at[me, core, rows]

        @pl.when(jnp.logical_not(local(j)))
        def _():
            remote(source, target, x.send_w, x.recv_w.at[me], workers[j], 2 * side).start()

        @pl.when(local(j))
        def _():
            pltpu.make_async_copy(source, target, x.recv_w.at[me]).start()

    def cut(k):
        arrived(slabs[k].at[pl.ds(0, stripe_count - 1)], x.recv_n.at[k])
        start, size = in_cuts[k]
        for j in order:
            owner, _, row, col = slot_of(capacity * side + j)
            later = lax.rem(owner + 1, stripe_count)
            here = rows_from(size) >= row - start
            near = cols_from(size) >= col
            left, mid, right = (
                jnp.where(
                    here,
                    slabs[k][owner, :, pl.ds(place * half, half)].astype(jnp.int32),
                    slabs[k][later, :, pl.ds(place * half, half)].astype(jnp.int32),
                )
                for place in range(3)
            )
            x.win[j, in_rows[k], pl.ds(0, half)] = jnp.where(near, left, right).astype(jnp.int16)
            x.win[j, in_rows[k], pl.ds(half, half)] = mid.astype(jnp.int16)

            if k == 0:
                @pl.when(me < workers[j])
                def _():
                    pl.semaphore_wait(x.ready.at[j], 1)

    def lag_cases(j):
        upper = me >= depth_count // 2
        other = lax.rem(me + workers[j], 2) == 1
        middle = (me >= depth_count // 4) & jnp.logical_not(upper) & (workers[j] >= depth_count // 2)
        held = upper & other
        plain = jnp.logical_not(held | middle)
        return [(0, plain), (UPPER_LAG, held), (MIDDLE_LAG, middle)]

    for step in range(ins + max(UPPER_LAG, MIDDLE_LAG)):
        if step < ins:
            with jax.named_scope(f"cut{step}"):
                cut(step)
        for j in order:
            for lag, here in lag_cases(j):
                if 0 <= step - lag < ins:
                    @pl.when(here)
                    def _():
                        window_send(j, in_rows[step - lag])

    @pl.when(in_plane)
    def _():
        for target in range(2):
            @pl.when(stripe == 2 * target)
            def _():
                pltpu.make_async_copy(x.amp_send.at[target], x.patterns.at[stripe], x.recv_a).start()

            @pl.when(stripe != 2 * target)
            def _():
                remote(
                    x.amp_send.at[target], x.patterns.at[stripe], x.send_a.at[target], x.recv_a, me, 2 * target
                ).start()

    def right_dot(value, which):
        high, low = parts_of(value)
        return dot(jnp.concatenate([high, high, low], axis=1), x.rstack[which])

    def left_dot(which, value):
        high, low = parts_of(value)
        return dot(x.lstack[which], jnp.concatenate([high, high, low], axis=0))

    def split_lanes(re, im):
        return (
            jnp.concatenate([re[:, :half] + re[:, half:], im[:, :half] + im[:, half:]], axis=1),
            jnp.concatenate([re[:, :half] - re[:, half:], im[:, :half] - im[:, half:]], axis=1),
        )

    def split_rows(re, im):
        return (
            jnp.concatenate([re[:half] + re[half:], im[:half] + im[half:]], axis=0),
            jnp.concatenate([re[:half] - re[half:], im[:half] - im[half:]], axis=0),
        )

    def join_lanes(p, q):
        return (
            jnp.concatenate([p[:, :half] + q[:, :half], p[:, :half] - q[:, :half]], axis=1),
            jnp.concatenate([p[:, half:] + q[:, half:], p[:, half:] - q[:, half:]], axis=1),
        )

    def join_rows(p, q):
        return (
            jnp.concatenate([p[:half] + q[:half], p[:half] - q[:half]], axis=0),
            jnp.concatenate([p[half:] + q[half:], p[half:] - q[half:]], axis=0),
        )

    def propagate(re, im):
        u, v = split_lanes(re, im)
        re, im = join_lanes(right_dot(u, 0), right_dot(v, 1))
        u, v = split_rows(re, im)
        return join_rows(left_dot(0, u), left_dot(1, v))

    def window_of(layer):
        value = x.wins[layer].astype(jnp.int32).astype(jnp.float32)
        return value[0], value[1]

    def gradient_copies(layer, k, action):
        for part in range(2):
            @pl.when((layer != me) | (part == 1))
            def _():
                action(
                    remote(
                        x.gout.at[2 * layer + part, out_rows[k]], x.gin.at[my_j, out_rows[k]], x.send_g,
                        x.recv_g.at[k], layer, 2 * side + part,
                    )
                )

        @pl.when(layer == me)
        def _():
            action(
                pltpu.make_async_copy(
                    x.gout.at[2 * layer, out_rows[k]], x.gin.at[my_j, out_rows[k]], x.recv_g.at[k]
                )
            )

    def emit(layer, re, im):
        for part, value in enumerate((re, im)):
            for k in range(outs):
                start, size = out_cuts[k]
                piece = value[start : start + size]
                most = jnp.maximum(jnp.max(jnp.abs(piece), axis=0, keepdims=True), 1e-30)
                x.gout[2 * layer + part, out_rows[k]] = jnp.round(piece * (LEVELS / most)).astype(jnp.int32).astype(jnp.int16)
                x.gscale[2 * layer + part, k] = most * (1.0 / LEVELS)

        def scale_copy(part):
            return remote(
                x.gscale.at[2 * layer + part], x.gin_scale.at[my_j], x.send_gs, x.recv_gs, layer,
                2 * side + part,
            )

        @pl.when(layer != me)
        def _():
            scale_copy(0).start()

        @pl.when(layer == me)
        def _():
            pltpu.make_async_copy(x.gscale.at[2 * layer], x.gin_scale.at[my_j], x.recv_gs).start()

        scale_copy(1).start()
        for k in range(outs):
            held = layer + k

            @pl.when((held < depth_count) & ((held >= LATE) | (k == 0)))
            def _():
                gradient_copies(held, k, lambda copy: copy.start())

    @pl.when(is_worker)
    def _():
        arrived(x.rstack, x.sem_r)
        arrived(x.lstack, x.sem_l)

        @pl.loop(0, depth_count - 1)
        def forward(layer):
            with jax.named_scope("fw_wait"):
                arrived(x.wins.at[layer], x.recv_w.at[layer])
            win_re, win_im = window_of(layer)
            re, im = x.waves[layer, 0], x.waves[layer, 1]
            re, im = propagate(re * win_re - im * win_im, re * win_im + im * win_re)
            x.waves[layer + 1, 0] = re
            x.waves[layer + 1, 1] = im

        last = depth_count - 1
        with jax.named_scope("last_wait"):
            arrived(x.wins.at[last], x.recv_w.at[last])
        win_re, win_im = window_of(last)
        wave_re, wave_im = x.waves[last, 0], x.waves[last, 1]
        re = (wave_re * win_re - wave_im * win_im) * (1.0 / LEVELS)
        im = (wave_re * win_im + wave_im * win_re) * (1.0 / LEVELS)
        u, v = split_lanes(re, im)
        even, odd = right_dot(u, 2), right_dot(v, 3)
        re = jnp.concatenate([even[:, :half], odd[:, :half]], axis=1)
        im = jnp.concatenate([even[:, half:], odd[:, half:]], axis=1)
        u, v = split_rows(re, im)
        even, odd = left_dot(2, u), left_dot(3, v)
        with jax.named_scope("amp_wait"):
            arrived(x.patterns, x.recv_a)
        amp = x.patterns[my_owner].astype(jnp.float32)
        re = jnp.concatenate([even[:half], odd[:half]], axis=0)
        im = jnp.concatenate([even[half:], odd[half:]], axis=0)
        factor = 1.0 - amp / jnp.sqrt(re * re + im * im + smoothing)
        re, im = factor * re, factor * im

        def left_back(which, value):
            high, low = parts_of(value)
            table = x.rstack[which, pl.ds(0, length)]
            table_low = x.rstack[which, pl.ds(length, length)]
            return dot(table, high) + dot(table_low, high) + dot(table, low)

        def right_back(value, which):
            high, low = parts_of(value)
            table = x.lstack[which, :, pl.ds(0, length)]
            table_low = x.lstack[which, :, pl.ds(length, length)]
            return dot(high, table) + dot(high, table_low) + dot(low, table)

        re, im = join_rows(
            left_back(2, jnp.concatenate([re[:half], im[:half]], axis=0)),
            left_back(3, jnp.concatenate([re[half:], im[half:]], axis=0)),
        )
        mid_re, mid_im = join_lanes(
            right_back(jnp.concatenate([re[:, :half], im[:, :half]], axis=1), 2),
            right_back(jnp.concatenate([re[:, half:], im[:, half:]], axis=1), 3),
        )
        emit(
            last,
            wave_re * mid_re + wave_im * mid_im,
            wave_re * mid_im - wave_im * mid_re,
        )
        x.adj[0] = win_re * mid_re + win_im * mid_im
        x.adj[1] = win_im * mid_re - win_re * mid_im

        @pl.loop(1, depth_count)
        def backward(step):
            layer = last - step
            with jax.named_scope("bw"):
                mid_re, mid_conj = propagate(x.adj[0], x.adj[1])
                win_re, win_im = window_of(layer)
                wave_re, wave_im = x.waves[layer, 0], x.waves[layer, 1]
                emit(
                    layer,
                    wave_re * mid_re - wave_im * mid_conj,
                    -(wave_re * mid_conj + wave_im * mid_re),
                )
                x.adj[0] = win_re * mid_re - win_im * mid_conj
                x.adj[1] = win_im * mid_re + win_re * mid_conj

        for k in range(1, outs):
            for layer in range(LATE):
                gradient_copies(layer, k, lambda copy: copy.start())

    def far_copy(cc, k):
        return remote(
            x.far.at[cc, out_rows[k]], x.given.at[core, out_rows[k]], x.send_f, x.recv_f.at[k], me, across + cc
        )

    def far_scale_copy(cc, k):
        return remote(
            x.far_scale.at[cc, k], x.given_scale.at[core, k], x.send_fs, x.recv_fs.at[k], me, across + cc
        )

    def mate_copy(k):
        return remote(x.mate.at[out_rows[k]], x.mate_in.at[out_rows[k]], x.send_m, x.recv_m.at[k], me, partner)

    def reduce_chunk(k):
        with jax.named_scope(f"gin_wait{k}"):
            if k == 0:
                arrived(x.gin_scale, x.recv_gs)
            arrived(x.gin.at[:, out_rows[k]], x.recv_g.at[k])
        start, size = out_cuts[k]
        targets = [stripe, partner, across, across + 1]
        sums = [[0.0] * 3 for _ in targets]
        for j in range(capacity):
            owner, _, row, col = slot_of(capacity * side + j)
            later = lax.rem(owner + 1, stripe_count)
            here = rows_from(size) >= row - start
            near = cols_from(size) >= col
            scale = x.gin_scale[j, k]
            left = x.gin[j, out_rows[k], pl.ds(0, half)].astype(jnp.int32).astype(jnp.float32) * scale[:, :half]
            mid = x.gin[j, out_rows[k], pl.ds(half, half)].astype(jnp.int32).astype(jnp.float32) * scale[:, half:]
            pieces = (jnp.where(near, left, 0.0), mid, jnp.where(near, 0.0, left))
            for t, target in enumerate(targets):
                gain = jnp.where(
                    here, jnp.where(owner == target, 1.0, 0.0), jnp.where(later == target, 1.0, 0.0)
                )
                for place, piece in enumerate(pieces):
                    sums[t][place] = sums[t][place] + piece * gain
        for cc in range(2):
            for place in range(3):
                lanes = pl.ds(place * half, half)
                total = sums[2 + cc][place]
                most = jnp.maximum(jnp.max(jnp.abs(total), axis=0, keepdims=True), 1e-30)
                x.far[cc, out_rows[k], lanes] = jnp.round(total * (LEVELS / most)).astype(jnp.int32).astype(jnp.int16)
                x.far_scale[cc, k, :, lanes] = most * (1.0 / LEVELS)
            far_copy(cc, k).start()
            far_scale_copy(cc, k).start()
        for place in range(3):
            lanes = pl.ds(place * half, half)
            x.mate[out_rows[k], lanes] = sums[1][place]
            x.own[out_rows[k], lanes] = sums[0][place]
        mate_copy(k).start()

    def finish_chunk(k):
        with jax.named_scope(f"far_wait{k}"):
            arrived(x.given.at[:, out_rows[k]], x.recv_f.at[k])
            arrived(x.given_scale.at[:, k], x.recv_fs.at[k])
            arrived(x.mate_in.at[out_rows[k]], x.recv_m.at[k])
        for part, base in ((core, x.own), (1 - core, x.mate_in)):
            value = x.given[part, out_rows[k]].astype(jnp.int32).astype(jnp.float32)
            out_ref[0, part, out_rows[k]] = base[out_rows[k]] + value * x.given_scale[part, k]

    for k in range(outs):
        reduce_chunk(k)
        if k > 0:
            finish_chunk(k - 1)
    finish_chunk(outs - 1)

    arrived(x.stage, x.send_n.at[0])
    arrived(x.stage.at[0], x.send_n.at[1])
    arrived(x.far, x.send_f)
    arrived(x.far_scale, x.send_fs)
    arrived(x.mate, x.send_m)
    @pl.when(is_worker)
    def _():
        arrived(x.win.at[pl.ds(0, capacity - 1)], x.send_w)

    @pl.when(jnp.logical_not(is_worker))
    def _():
        arrived(x.win, x.send_w)

    @pl.when(in_plane)
    def _():
        for target in range(2):
            @pl.when(stripe != 2 * target)
            def _():
                arrived(x.amp_send.at[target], x.send_a.at[target])

    @pl.when(is_worker)
    def _():
        arrived(x.gout.at[pl.ds(0, 2 * depth_count - 1)], x.send_g)
        arrived(x.gscale.at[pl.ds(0, 2 * depth_count - 1)], x.send_gs)


def body(tables, object_slices, probe_wave, amplitudes, positions, counts):
    stripe_count = lax.axis_size("stripe")
    depth_count = lax.axis_size("depth")
    layers, _, stripe_rows, width = object_slices.shape
    length = probe_wave.shape[1]
    capacity = amplitudes.shape[0]
    assert layers == 1 and stripe_rows == length and 2 * width == 3 * length
    assert depth_count % 8 == 0 and stripe_count == 4 and capacity == 4
    items = scratch_list(depth_count, stripe_count, capacity, length, width, tables.shape[0] - 2)
    sizes = (depth_count, stripe_count, capacity, length, width)
    held = sum(
        int(np.prod(shape.shape)) * jnp.dtype(shape.dtype).itemsize
        for _, shape in items
        if getattr(shape, "memory_space", None) == pltpu.VMEM
    )
    operands = (positions.T, counts, object_slices, probe_wave, amplitudes, tables)
    return pl.pallas_call(
        functools.partial(kernel, [name for name, _ in items], sizes),
        out_shape=pltpu.VMEM(object_slices.shape, jnp.float32),
        in_specs=[pl.BlockSpec(memory_space=pl.ANY)] * len(operands),
        out_specs=pl.BlockSpec(memory_space=pltpu.VMEM),
        scratch_shapes=[shape for _, shape in items],
        compiler_params=pltpu.CompilerParams(
            collective_id=0, has_side_effects=True, vmem_limit_bytes=held + (6 << 20)
        ),
    )(*(pltpu.with_memory_space_constraint(operand, pltpu.HBM) for operand in operands))


def solution(mesh):
    def run(object_slices, probe_wave, amplitudes, positions, counts):
        tables = jnp.asarray(make_tables(probe_wave.shape[1]))
        return jax.shard_map(
            body,
            mesh=mesh,
            in_specs=(P(), P("depth", None, "stripe", None), P(), P("stripe", None, None), P(), P()),
            out_specs=P("depth", None, "stripe", None),
            check_vma=False,
        )(tables, object_slices, probe_wave, amplitudes, positions, counts)

    return run
```

```python
import functools
import types

import jax
import jax.numpy as jnp
import numpy as np
from jax import lax
from jax.experimental import pallas as pl
from jax.experimental.pallas import tpu as pltpu
from jax.sharding import PartitionSpec as P

smoothing = 0.25
LEVELS = 32767.0
IN_CUTS = (48, 64, 80, 64)
OUT_CUTS = (64, 64, 64, 64)
LATE = 5
ORDER = (2, 3, 1, 0)
UPPER_LAG = 0
MIDDLE_LAG = 1
MESH = pl.DeviceIdType.MESH


def right_form(matrix):
    return np.block([[matrix.real, matrix.imag], [-matrix.imag, matrix.real]])


def make_tables(length):
    half = length // 2
    index = np.arange(length)
    dft = np.exp(-2j * np.pi * (np.outer(index, index) % length) / length) / np.sqrt(length)
    freq = (index + half) % length - half
    fresnel = np.exp(-1j * np.pi * freq.astype(np.float64) ** 2 / (2.0 * length))
    prop = dft.conj() @ (fresnel[:, None] * dft)
    first, second = prop[:half, :half], prop[:half, half:]
    parts = [(first + second) / 2, (first - second) / 2, dft[:half, 0::2], dft[:half, 1::2]]
    tables = []
    for place, part in enumerate(parts):
        right = right_form(part)
        tables += [right / LEVELS if place < 2 else right, right.T]
    stacked = np.stack(tables).astype(np.float32)
    high = stacked.astype(jnp.bfloat16)
    low = (stacked - high.astype(np.float32)).astype(jnp.bfloat16)
    order = np.concatenate([np.arange(0, length, 2), np.arange(1, length, 2)])
    pick = np.zeros((length, length), np.float32)
    pick[np.arange(length), order] = 1.0
    picks = np.stack([pick, pick.T]).astype(jnp.bfloat16)
    return np.concatenate([high, low, picks], axis=0)


def cut_rows(length, cuts):
    unit = length // sum(cuts)
    sizes = [size * unit for size in cuts]
    return [(sum(sizes[:k]), size) for k, size in enumerate(sizes)]


def worker_depths(depth_count):
    return [depth_count // 8, depth_count // 4, depth_count // 2, depth_count // 2 + 1]


def parts_of(value):
    high = value.astype(jnp.bfloat16)
    low = (value - high.astype(jnp.float32)).astype(jnp.bfloat16)
    return high, low


def dot(a, b):
    return jnp.dot(a, b, preferred_element_type=jnp.float32)


def scratch_list(depth_count, stripe_count, capacity, length, width, tables):
    dma, regular = pltpu.SemaphoreType.DMA, pltpu.SemaphoreType.REGULAR
    count = tables // 4
    ins, outs = len(IN_CUTS), len(OUT_CUTS)
    field = (2, length, length)
    items = [
        ("obj", pltpu.VMEM((2, length, width), jnp.float32)),
        ("stage", pltpu.VMEM((2, length, width), jnp.int16)),
        ("win", pltpu.VMEM((capacity, length, length), jnp.int16)),
        ("wins", pltpu.VMEM((depth_count,) + field, jnp.int16)),
        ("waves", pltpu.VMEM((depth_count,) + field, jnp.float32)),
        ("gout", pltpu.VMEM((2 * depth_count, length, length), jnp.int16)),
        ("gscale", pltpu.VMEM((2 * depth_count, outs, 1, length), jnp.float32)),
        ("gin", pltpu.VMEM((capacity, length, length), jnp.int16)),
        ("gin_scale", pltpu.VMEM((capacity, outs, 1, length), jnp.float32)),
        ("rstack", pltpu.VMEM((count, 3 * length, length), jnp.bfloat16)),
        ("lstack", pltpu.VMEM((count, length, 3 * length), jnp.bfloat16)),
        ("picks", pltpu.VMEM((2, length, length), jnp.bfloat16)),
        ("probe", pltpu.VMEM(field, jnp.bfloat16)),
        ("amp", pltpu.VMEM((capacity, length, length), jnp.bfloat16)),
        ("amp_send", pltpu.VMEM((2, length, length), jnp.bfloat16)),
        ("patterns", pltpu.VMEM((stripe_count, length, length), jnp.bfloat16)),
        ("adj", pltpu.VMEM(field, jnp.float32)),
        ("far", pltpu.VMEM((2, length, width), jnp.int16)),
        ("far_scale", pltpu.VMEM((2, outs, 1, width), jnp.float32)),
        ("given", pltpu.VMEM((2, length, width), jnp.int16)),
        ("given_scale", pltpu.VMEM((2, outs, 1, width), jnp.float32)),
        ("own", pltpu.VMEM((length, width), jnp.float32)),
        ("mate", pltpu.VMEM((length, width), jnp.float32)),
        ("mate_in", pltpu.VMEM((length, width), jnp.float32)),
        ("positions", pltpu.SMEM((2, stripe_count * capacity), jnp.int32)),
        ("counts", pltpu.SMEM((stripe_count,), jnp.int32)),
        ("sem_s", dma((2,))),
        ("sem_obj", dma((ins,))),
        ("sem_r", dma),
        ("sem_l", dma),
        ("sem_p", dma((3,))),
        ("ready", regular((capacity,))),
        ("send_n", dma((2,))),
        ("recv_n", dma((ins,))),
        ("send_w", dma),
        ("recv_w", dma((depth_count,))),
        ("send_a", dma((2,))),
        ("recv_a", dma),
        ("send_g", dma),
        ("send_gs", dma),
        ("recv_g", dma((outs,))),
        ("recv_gs", dma),
        ("send_f", dma),
        ("send_fs", dma),
        ("recv_f", dma((outs,))),
        ("recv_fs", dma((outs,))),
        ("send_m", dma),
        ("recv_m", dma((outs,))),
    ]
    for k, (_, size) in enumerate(cut_rows(length, IN_CUTS)):
        items.append((f"slab{k}", pltpu.VMEM((stripe_count, size, width), jnp.int16)))
    return items


def kernel(names, sizes, positions_hbm, counts_hbm, object_hbm, probe_hbm, amp_hbm, table_hbm, out_ref, *scratch):
    depth_count, stripe_count, capacity, length, width = sizes
    x = types.SimpleNamespace(**dict(zip(names, scratch, strict=True)))
    in_cuts, out_cuts = cut_rows(length, IN_CUTS), cut_rows(length, OUT_CUTS)
    ins, outs = len(in_cuts), len(out_cuts)
    in_rows = [pl.ds(start, size) for start, size in in_cuts]
    out_rows = [pl.ds(start, size) for start, size in out_cuts]
    slabs = [getattr(x, f"slab{k}") for k in range(ins)]
    half = length // 2
    count = x.rstack.shape[0]
    me, stripe = lax.axis_index("depth"), lax.axis_index("stripe")
    core, side = lax.rem(stripe, 2), stripe // 2
    partner = stripe + 1 - 2 * core
    across = lax.rem(2 * side + 2, stripe_count)
    workers = worker_depths(depth_count)
    in_plane = functools.reduce(jnp.logical_or, [me == worker for worker in workers])
    my_j = sum(jnp.where(me == worker, j, 0) for j, worker in enumerate(workers))
    is_worker = in_plane & (core == 0)

    def remote(src, dst, send, recv, depth, where):
        return pltpu.make_async_remote_copy(
            src_ref=src, dst_ref=dst, send_sem=send, recv_sem=recv, device_id=(depth, where), device_id_type=MESH
        )

    def arrived(ref, sem):
        pltpu.make_async_copy(ref, ref, sem).wait()

    def slot_of(place):
        owner, passed, start = jnp.int32(0), jnp.int32(0), jnp.int32(0)
        for other in range(1, stripe_count):
            passed = passed + x.counts[other - 1]
            owner = owner + jnp.where(place >= passed, 1, 0)
            start = jnp.where(place >= passed, passed, start)
        within = jnp.clip(place - start, 0, capacity - 1)
        slot = owner * capacity + within
        return owner, within, x.positions[0, slot], x.positions[1, slot]

    def scalar_loads():
        return [
            pltpu.make_async_copy(positions_hbm, x.positions, x.sem_s.at[0]),
            pltpu.make_async_copy(counts_hbm, x.counts, x.sem_s.at[1]),
        ]

    for k in range(ins):
        pltpu.make_async_copy(object_hbm.at[0, :, in_rows[k]], x.obj.at[:, in_rows[k]], x.sem_obj.at[k]).start()

    for copy in scalar_loads():
        copy.start()

    barrier = pltpu.get_barrier_semaphore()
    for step in range(1, stripe_count):
        other = lax.rem(stripe + step, stripe_count)
        pl.semaphore_signal(barrier, inc=1, device_id=(me, other), device_id_type=MESH)

    @pl.when(is_worker)
    def _():
        @pl.loop(me + 1, depth_count)
        def _(layer):
            for cc in range(2):
                pl.semaphore_signal(barrier, inc=1, device_id=(layer, 2 * side + cc), device_id_type=MESH)

    @pl.when(jnp.logical_not(is_worker))
    def _():
        for worker in workers:
            @pl.when(me < worker)
            def _():
                pl.semaphore_signal(barrier, inc=1, device_id=(worker, 2 * side), device_id_type=MESH)

    @pl.when(in_plane)
    def _():
        pltpu.make_async_copy(amp_hbm, x.amp, x.sem_p.at[0]).start()
        pltpu.make_async_copy(table_hbm.at[pl.ds(4 * count, 2)], x.picks, x.sem_p.at[1]).start()

    @pl.when(is_worker)
    def _():
        pltpu.make_async_copy(probe_hbm, x.probe, x.sem_p.at[2]).start()
        for which in range(count):
            high, low = 2 * which, 2 * count + 2 * which
            for place, source in enumerate((high, low, high)):
                span = pl.ds(place * length, length)
                pltpu.make_async_copy(table_hbm.at[source], x.rstack.at[which, span], x.sem_r).start()
                pltpu.make_async_copy(table_hbm.at[source + 1], x.lstack.at[which, :, span], x.sem_l).start()

    def quantize(k):
        pltpu.make_async_copy(object_hbm.at[0, :, in_rows[k]], x.obj.at[:, in_rows[k]], x.sem_obj.at[k]).wait()
        for part in range(2):
            whole = jnp.round(x.obj[part, in_rows[k]] * LEVELS).astype(jnp.int32).astype(jnp.int16)
            x.stage[part, in_rows[k]] = whole
        slabs[k][stripe] = x.stage[core, in_rows[k]]

    def spread(k):
        for cc in range(2):
            remote(
                x.stage.at[cc, in_rows[k]], slabs[k].at[stripe], x.send_n.at[0], x.recv_n.at[k], me, across + cc
            ).start()
        remote(
            x.stage.at[1 - core, in_rows[k]], slabs[k].at[stripe], x.send_n.at[1], x.recv_n.at[k], me, partner
        ).start()

    quantize(0)
    with jax.named_scope("barrier"):
        lower_workers = sum(jnp.where(worker < me, 1, 0) for worker in workers)
        pl.semaphore_wait(barrier, stripe_count - 1 + jnp.where(is_worker, 2 * me, lower_workers))

    @pl.when(is_worker)
    def _():
        @pl.loop(0, me)
        def _(layer):
            for cc in range(2):
                pl.semaphore_signal(x.ready.at[my_j], inc=1, device_id=(layer, 2 * side + cc), device_id_type=MESH)

    for k in range(ins):
        if k > 0:
            quantize(k)
        spread(k)

    for copy in scalar_loads():
        copy.wait()

    @pl.when(in_plane)
    def _():
        pltpu.make_async_copy(amp_hbm, x.amp, x.sem_p.at[0]).wait()
        pltpu.make_async_copy(table_hbm.at[pl.ds(4 * count, 2)], x.picks, x.sem_p.at[1]).wait()
        for target in range(2):
            _, within, _, _ = slot_of(capacity * target + my_j)
            moved = dot(x.picks[0], x.amp[within]).astype(jnp.bfloat16)
            x.amp_send[target] = dot(moved, x.picks[1]).astype(jnp.bfloat16)

    my_owner, _, my_row, my_col = slot_of(capacity * side + my_j)

    @pl.when(is_worker)
    def _():
        pltpu.make_async_copy(probe_hbm, x.probe, x.sem_p.at[2]).wait()
        first = lax.broadcasted_iota(jnp.int32, (length, length), 0)
        second = lax.broadcasted_iota(jnp.int32, (length, length), 1)
        turned = second + my_row
        turned = jnp.where(turned >= length, turned - length, turned)
        turn_rows = jnp.where(first == turned, 1.0, 0.0).astype(jnp.bfloat16)
        turned = first + my_col
        turned = jnp.where(turned >= length, turned - length, turned)
        turn_cols = jnp.where(second == turned, 1.0, 0.0).astype(jnp.bfloat16)
        for part in range(2):
            value = dot(turn_rows, x.probe[part]).astype(jnp.bfloat16)
            x.waves[0, part] = dot(value, turn_cols)

    def rows_from(size):
        return lax.broadcasted_iota(jnp.int32, (size, half), 0)

    def cols_from(size):
        return lax.broadcasted_iota(jnp.int32, (size, half), 1)

    order = ORDER

    def local(j):
        return (me == workers[j]) & (core == 0)

    def window_send(j, rows):
        source, target = x.win.at[j, rows], x.wins.at[me, core, rows]

        @pl.when(jnp.logical_not(local(j)))
        def _():
            remote(source, target, x.send_w, x.recv_w.at[me], workers[j], 2 * side).start()

        @pl.when(local(j))
        def _():
            pltpu.make_async_copy(source, target, x.recv_w.at[me]).start()

    def cut(k):
        arrived(slabs[k].at[pl.ds(0, stripe_count - 1)], x.recv_n.at[k])
        start, size = in_cuts[k]
        for j in order:
            owner, _, row, col = slot_of(capacity * side + j)
            later = lax.rem(owner + 1, stripe_count)
            here = rows_from(size) >= row - start
            near = cols_from(size) >= col
            left, mid, right = (
                jnp.where(
                    here,
                    slabs[k][owner, :, pl.ds(place * half, half)].astype(jnp.int32),
                    slabs[k][later, :, pl.ds(place * half, half)].astype(jnp.int32),
                )
                for place in range(3)
            )
            x.win[j, in_rows[k], pl.ds(0, half)] = jnp.where(near, left, right).astype(jnp.int16)
            x.win[j, in_rows[k], pl.ds(half, half)] = mid.astype(jnp.int16)

            if k == 0:
                @pl.when(me < workers[j])
                def _():
                    pl.semaphore_wait(x.ready.at[j], 1)

    def lag_cases(j):
        upper = me >= depth_count // 2
        other = lax.rem(me + workers[j], 2) == 1
        middle = (me >= depth_count // 4) & jnp.logical_not(upper) & (workers[j] >= depth_count // 2)
        held = upper & other
        plain = jnp.logical_not(held | middle)
        return [(0, plain), (UPPER_LAG, held), (MIDDLE_LAG, middle)]

    for step in range(ins + max(UPPER_LAG, MIDDLE_LAG)):
        if step < ins:
            with jax.named_scope(f"cut{step}"):
                cut(step)
        for j in order:
            for lag, here in lag_cases(j):
                if 0 <= step - lag < ins:
                    @pl.when(here)
                    def _():
                        window_send(j, in_rows[step - lag])

    @pl.when(in_plane)
    def _():
        for target in range(2):
            @pl.when(stripe == 2 * target)
            def _():
                pltpu.make_async_copy(x.amp_send.at[target], x.patterns.at[stripe], x.recv_a).start()

            @pl.when(stripe != 2 * target)
            def _():
                remote(
                    x.amp_send.at[target], x.patterns.at[stripe], x.send_a.at[target], x.recv_a, me, 2 * target
                ).start()

    def right_dot(value, which):
        high, low = parts_of(value)
        return dot(jnp.concatenate([high, high, low], axis=1), x.rstack[which])

    def left_dot(which, value):
        high, low = parts_of(value)
        return dot(x.lstack[which], jnp.concatenate([high, high, low], axis=0))

    def split_lanes(re, im):
        return (
            jnp.concatenate([re[:, :half] + re[:, half:], im[:, :half] + im[:, half:]], axis=1),
            jnp.concatenate([re[:, :half] - re[:, half:], im[:, :half] - im[:, half:]], axis=1),
        )

    def split_rows(re, im):
        return (
            jnp.concatenate([re[:half] + re[half:], im[:half] + im[half:]], axis=0),
            jnp.concatenate([re[:half] - re[half:], im[:half] - im[half:]], axis=0),
        )

    def join_lanes(p, q):
        return (
            jnp.concatenate([p[:, :half] + q[:, :half], p[:, :half] - q[:, :half]], axis=1),
            jnp.concatenate([p[:, half:] + q[:, half:], p[:, half:] - q[:, half:]], axis=1),
        )

    def join_rows(p, q):
        return (
            jnp.concatenate([p[:half] + q[:half], p[:half] - q[:half]], axis=0),
            jnp.concatenate([p[half:] + q[half:], p[half:] - q[half:]], axis=0),
        )

    def propagate(re, im):
        u, v = split_lanes(re, im)
        re, im = join_lanes(right_dot(u, 0), right_dot(v, 1))
        u, v = split_rows(re, im)
        return join_rows(left_dot(0, u), left_dot(1, v))

    def window_of(layer):
        value = x.wins[layer].astype(jnp.int32).astype(jnp.float32)
        return value[0], value[1]

    def gradient_copies(layer, k, action):
        for part in range(2):
            @pl.when((layer != me) | (part == 1))
            def _():
                action(
                    remote(
                        x.gout.at[2 * layer + part, out_rows[k]], x.gin.at[my_j, out_rows[k]], x.send_g,
                        x.recv_g.at[k], layer, 2 * side + part,
                    )
                )

        @pl.when(layer == me)
        def _():
            action(
                pltpu.make_async_copy(
                    x.gout.at[2 * layer, out_rows[k]], x.gin.at[my_j, out_rows[k]], x.recv_g.at[k]
                )
            )

    def emit(layer, re, im):
        for part, value in enumerate((re, im)):
            for k in range(outs):
                start, size = out_cuts[k]
                piece = value[start : start + size]
                most = jnp.maximum(jnp.max(jnp.abs(piece), axis=0, keepdims=True), 1e-30)
                x.gout[2 * layer + part, out_rows[k]] = jnp.round(piece * (LEVELS / most)).astype(jnp.int32).astype(jnp.int16)
                x.gscale[2 * layer + part, k] = most * (1.0 / LEVELS)

        def scale_copy(part):
            return remote(
                x.gscale.at[2 * layer + part], x.gin_scale.at[my_j], x.send_gs, x.recv_gs, layer,
                2 * side + part,
            )

        @pl.when(layer != me)
        def _():
            scale_copy(0).start()

        @pl.when(layer == me)
        def _():
            pltpu.make_async_copy(x.gscale.at[2 * layer], x.gin_scale.at[my_j], x.recv_gs).start()

        scale_copy(1).start()
        for k in range(outs):
            held = layer + k

            @pl.when((held < depth_count) & ((held >= LATE) | (k == 0)))
            def _():
                gradient_copies(held, k, lambda copy: copy.start())

    @pl.when(is_worker)
    def _():
        arrived(x.rstack, x.sem_r)
        arrived(x.lstack, x.sem_l)

        @pl.loop(0, depth_count - 1)
        def forward(layer):
            with jax.named_scope("fw_wait"):
                arrived(x.wins.at[layer], x.recv_w.at[layer])
            win_re, win_im = window_of(layer)
            re, im = x.waves[layer, 0], x.waves[layer, 1]
            re, im = propagate(re * win_re - im * win_im, re * win_im + im * win_re)
            x.waves[layer + 1, 0] = re
            x.waves[layer + 1, 1] = im

        last = depth_count - 1
        with jax.named_scope("last_wait"):
            arrived(x.wins.at[last], x.recv_w.at[last])
        win_re, win_im = window_of(last)
        wave_re, wave_im = x.waves[last, 0], x.waves[last, 1]
        re = (wave_re * win_re - wave_im * win_im) * (1.0 / LEVELS)
        im = (wave_re * win_im + wave_im * win_re) * (1.0 / LEVELS)
        u, v = split_lanes(re, im)
        even, odd = right_dot(u, 2), right_dot(v, 3)
        re = jnp.concatenate([even[:, :half], odd[:, :half]], axis=1)
        im = jnp.concatenate([even[:, half:], odd[:, half:]], axis=1)
        u, v = split_rows(re, im)
        even, odd = left_dot(2, u), left_dot(3, v)
        with jax.named_scope("amp_wait"):
            arrived(x.patterns, x.recv_a)
        amp = x.patterns[my_owner].astype(jnp.float32)
        re = jnp.concatenate([even[:half], odd[:half]], axis=0)
        im = jnp.concatenate([even[half:], odd[half:]], axis=0)
        factor = 1.0 - amp / jnp.sqrt(re * re + im * im + smoothing)
        re, im = factor * re, factor * im

        def left_back(which, value):
            high, low = parts_of(value)
            table = x.rstack[which, pl.ds(0, length)]
            table_low = x.rstack[which, pl.ds(length, length)]
            return dot(table, high) + dot(table_low, high) + dot(table, low)

        def right_back(value, which):
            high, low = parts_of(value)
            table = x.lstack[which, :, pl.ds(0, length)]
            table_low = x.lstack[which, :, pl.ds(length, length)]
            return dot(high, table) + dot(high, table_low) + dot(low, table)

        re, im = join_rows(
            left_back(2, jnp.concatenate([re[:half], im[:half]], axis=0)),
            left_back(3, jnp.concatenate([re[half:], im[half:]], axis=0)),
        )
        mid_re, mid_im = join_lanes(
            right_back(jnp.concatenate([re[:, :half], im[:, :half]], axis=1), 2),
            right_back(jnp.concatenate([re[:, half:], im[:, half:]], axis=1), 3),
        )
        emit(
            last,
            wave_re * mid_re + wave_im * mid_im,
            wave_re * mid_im - wave_im * mid_re,
        )
        x.adj[0] = win_re * mid_re + win_im * mid_im
        x.adj[1] = win_im * mid_re - win_re * mid_im

        @pl.loop(1, depth_count)
        def backward(step):
            layer = last - step
            with jax.named_scope("bw"):
                mid_re, mid_conj = propagate(x.adj[0], x.adj[1])
                win_re, win_im = window_of(layer)
                wave_re, wave_im = x.waves[layer, 0], x.waves[layer, 1]
                emit(
                    layer,
                    wave_re * mid_re - wave_im * mid_conj,
                    -(wave_re * mid_conj + wave_im * mid_re),
                )
                x.adj[0] = win_re * mid_re - win_im * mid_conj
                x.adj[1] = win_im * mid_re + win_re * mid_conj

        for k in range(1, outs):
            for layer in range(LATE):
                gradient_copies(layer, k, lambda copy: copy.start())

    def far_copy(cc, k):
        return remote(
            x.far.at[cc, out_rows[k]], x.given.at[core, out_rows[k]], x.send_f, x.recv_f.at[k], me, across + cc
        )

    def far_scale_copy(cc, k):
        return remote(
            x.far_scale.at[cc, k], x.given_scale.at[core, k], x.send_fs, x.recv_fs.at[k], me, across + cc
        )

    def mate_copy(k):
        return remote(x.mate.at[out_rows[k]], x.mate_in.at[out_rows[k]], x.send_m, x.recv_m.at[k], me, partner)

    def reduce_chunk(k):
        with jax.named_scope(f"gin_wait{k}"):
            if k == 0:
                arrived(x.gin_scale, x.recv_gs)
            arrived(x.gin.at[:, out_rows[k]], x.recv_g.at[k])
        start, size = out_cuts[k]
        terms = []
        for j in range(capacity):
            owner, _, row, col = slot_of(capacity * side + j)
            later = lax.rem(owner + 1, stripe_count)
            here = rows_from(size) >= row - start
            near = cols_from(size) >= col
            scale = x.gin_scale[j, k]
            left = x.gin[j, out_rows[k], pl.ds(0, half)].astype(jnp.int32).astype(jnp.float32) * scale[:, :half]
            mid = x.gin[j, out_rows[k], pl.ds(half, half)].astype(jnp.int32).astype(jnp.float32) * scale[:, half:]
            terms.append((owner, later, here, (jnp.where(near, left, 0.0), mid, jnp.where(near, 0.0, left))))

        def sums_for(target):
            sums = [0.0] * 3
            for owner, later, here, pieces in terms:
                gain = jnp.where(
                    here, jnp.where(owner == target, 1.0, 0.0), jnp.where(later == target, 1.0, 0.0)
                )
                for place, piece in enumerate(pieces):
                    sums[place] = sums[place] + piece * gain
            return sums

        for cc in range(2):
            for place, total in enumerate(sums_for(across + cc)):
                lanes = pl.ds(place * half, half)
                most = jnp.maximum(jnp.max(jnp.abs(total), axis=0, keepdims=True), 1e-30)
                x.far[cc, out_rows[k], lanes] = jnp.round(total * (LEVELS / most)).astype(jnp.int32).astype(jnp.int16)
                x.far_scale[cc, k, :, lanes] = most * (1.0 / LEVELS)
            far_copy(cc, k).start()
            far_scale_copy(cc, k).start()
        for place, total in enumerate(sums_for(partner)):
            x.mate[out_rows[k], pl.ds(place * half, half)] = total
        mate_copy(k).start()
        for place, total in enumerate(sums_for(stripe)):
            x.own[out_rows[k], pl.ds(place * half, half)] = total

    def finish_chunk(k):
        with jax.named_scope(f"far_wait{k}"):
            arrived(x.given.at[:, out_rows[k]], x.recv_f.at[k])
            arrived(x.given_scale.at[:, k], x.recv_fs.at[k])
            arrived(x.mate_in.at[out_rows[k]], x.recv_m.at[k])
        for part, base in ((core, x.own), (1 - core, x.mate_in)):
            value = x.given[part, out_rows[k]].astype(jnp.int32).astype(jnp.float32)
            out_ref[0, part, out_rows[k]] = base[out_rows[k]] + value * x.given_scale[part, k]

    for k in range(outs):
        reduce_chunk(k)
    for k in range(outs):
        finish_chunk(k)

    arrived(x.stage, x.send_n.at[0])
    arrived(x.stage.at[0], x.send_n.at[1])
    arrived(x.far, x.send_f)
    arrived(x.far_scale, x.send_fs)
    arrived(x.mate, x.send_m)
    @pl.when(is_worker)
    def _():
        arrived(x.win.at[pl.ds(0, capacity - 1)], x.send_w)

    @pl.when(jnp.logical_not(is_worker))
    def _():
        arrived(x.win, x.send_w)

    @pl.when(in_plane)
    def _():
        for target in range(2):
            @pl.when(stripe != 2 * target)
            def _():
                arrived(x.amp_send.at[target], x.send_a.at[target])

    @pl.when(is_worker)
    def _():
        arrived(x.gout.at[pl.ds(0, 2 * depth_count - 1)], x.send_g)
        arrived(x.gscale.at[pl.ds(0, 2 * depth_count - 1)], x.send_gs)


def body(tables, object_slices, probe_wave, amplitudes, positions, counts):
    stripe_count = lax.axis_size("stripe")
    depth_count = lax.axis_size("depth")
    layers, _, stripe_rows, width = object_slices.shape
    length = probe_wave.shape[1]
    capacity = amplitudes.shape[0]
    assert layers == 1 and stripe_rows == length and 2 * width == 3 * length
    assert depth_count % 8 == 0 and stripe_count == 4 and capacity == 4
    items = scratch_list(depth_count, stripe_count, capacity, length, width, tables.shape[0] - 2)
    sizes = (depth_count, stripe_count, capacity, length, width)
    held = sum(
        int(np.prod(shape.shape)) * jnp.dtype(shape.dtype).itemsize
        for _, shape in items
        if getattr(shape, "memory_space", None) == pltpu.VMEM
    )
    operands = (positions.T, counts, object_slices, probe_wave, amplitudes, tables)
    return pl.pallas_call(
        functools.partial(kernel, [name for name, _ in items], sizes),
        out_shape=pltpu.VMEM(object_slices.shape, jnp.float32),
        in_specs=[pl.BlockSpec(memory_space=pl.ANY)] * len(operands),
        out_specs=pl.BlockSpec(memory_space=pltpu.VMEM),
        scratch_shapes=[shape for _, shape in items],
        compiler_params=pltpu.CompilerParams(
            collective_id=0, has_side_effects=True, vmem_limit_bytes=held + (6 << 20)
        ),
    )(*(pltpu.with_memory_space_constraint(operand, pltpu.HBM) for operand in operands))


def solution(mesh):
    def run(object_slices, probe_wave, amplitudes, positions, counts):
        tables = jnp.asarray(make_tables(probe_wave.shape[1]))
        return jax.shard_map(
            body,
            mesh=mesh,
            in_specs=(P(), P("depth", None, "stripe", None), P(), P("stripe", None, None), P(), P()),
            out_specs=P("depth", None, "stripe", None),
            check_vma=False,
        )(tables, object_slices, probe_wave, amplitudes, positions, counts)

    return run
```
